256 devices in a mesh: depth: 64 (over x, z, core), strip: 4 (over y).
Axes of the slice: x: 4, y: 4, z: 8, core: 2. Of those that a mesh axis runs over, the one named last changes fastest.
Arguments:
- density: bfloat16 [256, 64, 1024], P('depth', 'strip'), may hold values from -6 to 6
- tf_bins: int32 [256, 64, 1024], P('depth', 'strip'), may hold values from 0 to 15
- tf_table: float32 [4, 16], replicated, may hold values from 0.2 to 2
- brick_order: int32 [4, 64], P('strip'), may hold values from 0 to 63, each once within a row
Outputs:
- image: float32 [4, 65536], P(None, ('strip', 'depth'))
The draws below stay inside these ranges and needn't reach their ends.
Inputs may be any that keep to these rules, and one draw needn't show every extreme that they name: `tf_bins`: each voxel's bin indexes a column of tf_table. `brick_order`: each row lists every brick once.
All inputs are finite; a program needn't handle non-finite values.
Results may differ from the reference program's by a relative error of at most 0.0017.
Values may be sent and summed in bfloat16 or wider, within the bound.
A program may use at most 64 MiB of HBM per device.

```python
import math
import jax
import jax.numpy as jnp
from jax import lax

PLANES = 4
ROWS_DEV = 16
NX = 1024
CLASSES = 16
BRICKS = 64
STRIPS = 4
NZ = 256
IMG_ROWS = 64


def touch_ends(entries, rng, low, high):
    extent = entries.shape
    spot = [jax.random.randint(jax.random.fold_in(rng, axis), (), 0, extent[axis]) for axis in range(len(extent))]
    entries = entries.at[tuple(spot)].set(low)
    longest = extent.index(max(extent))
    spot[longest] = (spot[longest] + 1) % extent[longest]
    return entries.at[tuple(spot)].set(high)


def levels(rng, dims, pieces, low, top_value):
    gain, own = 1.0, jax.random.fold_in(rng, 6)
    for dim, blocks in pieces:
        heights = jnp.exp(jax.random.uniform(jax.random.fold_in(own, dim), (blocks,), jnp.float32, low / len(pieces), top_value / len(pieces)))
        gain = gain * jnp.repeat(heights, dims[dim] // blocks).reshape([-1 if axis == dim else 1 for axis in range(len(dims))])
    return gain


def scatter_about(rng, extent, spread, limit, split=(), kind=jnp.bfloat16):
    entries = spread * jax.random.normal(rng, extent, jnp.float32)
    if split:
        entries = entries * levels(rng, extent, split, -0.22, 0.18)
    return jnp.clip(entries, -limit, limit).astype(kind)


def setup_inputs(seed: int = 0) -> dict:
    splits = jax.random.split(jax.random.key(seed), 5)
    density = scatter_about(splits[0], (NZ, IMG_ROWS, NX), 1.0, 6.0, ((0, 64), (1, 4)))
    tf_bins = touch_ends(jax.random.randint(splits[1], (NZ, IMG_ROWS, NX), 0, CLASSES), jax.random.fold_in(splits[1], 1), 0, CLASSES - 1).astype(jnp.int32)
    tf_table = jnp.clip(jnp.exp(jax.random.uniform(splits[2], (4, CLASSES), jnp.float32, math.log(0.2), math.log(2.0))), 0.2, 2.0)
    brick_order = jax.vmap(lambda own: jax.random.permutation(own, BRICKS))(jax.random.split(splits[3], STRIPS)).reshape((STRIPS, BRICKS)).astype(jnp.int32)
    return {"density": density, "tf_bins": tf_bins, "tf_table": tf_table, "brick_order": brick_order}


LIGHT_X = 0.36
LIGHT_Y = 0.48
LIGHT_Z = 0.8
SHADE_GAIN = 1.5

def shear_plane(values, plane_index):
    across = values.shape[-1]
    offset = (3 * plane_index // 8).astype(jnp.int32)
    fraction = (3 * plane_index % 8).astype(jnp.float32) / 8.0
    columns = jnp.arange(across, dtype=jnp.int32)
    first = jnp.where(columns < across - offset, jnp.roll(values, -offset, axis=2), 0.0)
    second = jnp.where(columns < across - offset - 1, jnp.roll(first, -1, axis=2), 0.0)
    return (1.0 - fraction) * first + fraction * second

def plane_terms(window, tf_plane, tf_table, plane_index, total_planes):
    beneath = window[0]
    middle = window[1]
    overhead = window[2]
    centre = middle[1:-1]
    sideways = jnp.pad(centre, ((0, 0), (1, 1)))
    slope_across = 0.5 * (sideways[:, 2:] - sideways[:, :-2])
    slope_down = 0.5 * (middle[2:] - middle[:-2])
    slope_deep = 0.5 * (overhead[1:-1] - beneath[1:-1])
    lengths = jnp.sqrt(1.0 + slope_across * slope_across + slope_down * slope_down + slope_deep * slope_deep)
    shading = (LIGHT_X * slope_across + LIGHT_Y * slope_down + LIGHT_Z * slope_deep) / lengths
    classes = jnp.arange(tf_table.shape[1], dtype=jnp.int32)
    onehot = (tf_plane[None, :, :] == classes[:, None, None]).astype(jnp.float32)
    looked = jnp.einsum('cm,myx->cyx', tf_table, onehot, precision=lax.Precision.HIGHEST)
    extinction = looked[0] * (1.0 + centre * centre) / total_planes
    opacity = 1.0 - jnp.exp(-extinction)
    emitted = looked[1:] * (opacity * jnp.exp(SHADE_GAIN * shading))[None]
    return shear_plane(jnp.concatenate([extinction[None], emitted], axis=0), plane_index)

def brick_terms(block, tf_brick, tf_table, first_plane, total_planes):
    height = block.shape[1] - 2
    across = block.shape[2]

    def advance(running, plane_at):
        colour, depth_sum = running
        window = lax.dynamic_slice_in_dim(block, plane_at, 3, 0)
        tf_plane = lax.dynamic_index_in_dim(tf_brick, plane_at, 0, keepdims=False)
        sheared = plane_terms(window, tf_plane, tf_table, first_plane + plane_at, total_planes)
        colour = colour + jnp.exp(-depth_sum)[None] * sheared[1:]
        depth_sum = depth_sum + sheared[0]
        return ((colour, depth_sum), None)
    start = (jnp.zeros((3, height, across), jnp.float32), jnp.zeros((height, across), jnp.float32))
    finished, ignored = lax.scan(advance, start, jnp.arange(tf_brick.shape[0], dtype=jnp.int32))
    return finished

def order_mask(sequence):
    bricks = sequence.shape[0]
    slots = jnp.arange(bricks, dtype=jnp.int32)
    onehot = (sequence[:, None] == slots[None, :]).astype(jnp.int32)
    position = lax.optimization_barrier(jnp.sum(onehot * slots[:, None], axis=0))
    return (position[None, :] < position[:, None]).astype(jnp.float32)

def reference(density, tf_bins, tf_table, brick_order):
    padded = jnp.pad(density, ((1, 1), (1, 1), (0, 0)))

    def one_brick(brick):
        first_plane = (brick * PLANES).astype(jnp.int32)
        block = lax.dynamic_slice_in_dim(padded, first_plane, PLANES + 2, 0).astype(jnp.float32)
        tf_brick = lax.dynamic_slice_in_dim(tf_bins, first_plane, PLANES, 0)
        colour, depth_sum = brick_terms(block, tf_brick, tf_table, first_plane, NZ)
        return jnp.concatenate([colour, depth_sum[None]], axis=0)
    layers = lax.map(one_brick, jnp.arange(BRICKS, dtype=jnp.int32))

    def one_strip(strip):
        rows_block = lax.dynamic_slice_in_dim(layers, (strip * ROWS_DEV).astype(jnp.int32), ROWS_DEV, 2)
        before = order_mask(lax.dynamic_index_in_dim(brick_order, strip, 0, keepdims=False))
        depths = rows_block[:, 3]
        prefix = jnp.einsum('ab,byx->ayx', before, depths, precision=lax.Precision.HIGHEST)
        weight = jnp.exp(-prefix)
        shown = lax.optimization_barrier(jnp.sum(weight[:, None] * rows_block[:, :3], axis=0))
        remaining = jnp.exp(-lax.optimization_barrier(jnp.sum(depths, axis=0)))
        return jnp.concatenate([shown, remaining[None]], axis=0)
    strips = lax.map(one_strip, jnp.arange(STRIPS, dtype=jnp.int32))
    return jnp.transpose(strips, (1, 0, 2, 3)).reshape(4, IMG_ROWS * NX)
```

```python
import functools

import jax
import jax.numpy as jnp
from jax import lax
from jax.experimental import pallas as pl
from jax.experimental.pallas import tpu as pltpu
from jax.sharding import PartitionSpec as P

LIGHT_X = 0.36
LIGHT_Y = 0.48
LIGHT_Z = 0.8
SHADE_GAIN = 1.5
MESH = pl.DeviceIdType.MESH
LANES = 128
SUB = 8
F32 = jnp.float32


def kernel(
    bricks, strips, planes, height, across, classes,
    dens_hbm, bins_hbm, table_hbm, order_hbm, out_ref,
    dens_v, bins_v, table_v, order_s, tab, field, rows_out, rows_in, plane_in,
    part_a, part_q, near, far, depth, wide, packed, arrived,
    in_sem, halo_send, halo_recv, tile_send, tile_recv,
):
    me = lax.axis_index("depth")
    strip = lax.axis_index("strip")
    tiles = across // LANES
    halves = height // SUB
    per_owner = height * tiles // bricks
    rows_msg = 4 * per_owner

    barrier = pltpu.get_barrier_semaphore()

    def greet(step, carry):
        pl.semaphore_signal(
            barrier, inc=1, device_id={"depth": lax.rem(me + step, bricks)}, device_id_type=MESH
        )
        return carry

    lax.fori_loop(1, bricks, greet, 0)

    @pl.when(strip > 0)
    def _():
        pl.semaphore_signal(barrier, inc=1, device_id={"strip": strip - 1}, device_id_type=MESH)

    @pl.when(strip < strips - 1)
    def _():
        pl.semaphore_signal(barrier, inc=1, device_id={"strip": strip + 1}, device_id_type=MESH)

    loads = [
        pltpu.make_async_copy(dens_hbm, dens_v, in_sem.at[0]),
        pltpu.make_async_copy(bins_hbm, bins_v, in_sem.at[1]),
        pltpu.make_async_copy(table_hbm, table_v, in_sem.at[2]),
        pltpu.make_async_copy(order_hbm, order_s, in_sem.at[3]),
    ]
    for load in loads:
        load.start()

    loads[0].wait()
    for p in range(planes):
        for t in range(tiles):
            field[p + 1, t, SUB : SUB + height, :] = dens_v[
                p, :, t * LANES : (t + 1) * LANES
            ].astype(F32)
    for p in range(planes):
        for t in range(tiles):
            rows_out[0, p, t : t + 1, :] = field[p + 1, t, SUB : SUB + 1, :]
            rows_out[1, p, t : t + 1, :] = field[p + 1, t, SUB + height - 1 : SUB + height, :]
    loads[2].wait()
    tab[0:4, 0:classes] = table_v[...]
    loads[1].wait()

    lane = lax.broadcasted_iota(jnp.int32, (SUB, LANES), 1)
    zero = jnp.zeros((SUB, LANES), F32)
    columns = [jnp.broadcast_to(tab[c : c + 1, :], (SUB, LANES)) for c in range(4)]
    depth[...] = jnp.zeros_like(depth)

    def shear_of(p):
        scaled = 3 * (me * planes + p)
        offset = scaled // 8
        fraction = (scaled % 8).astype(F32) * 0.125
        return offset, fraction

    def plane_terms(p, carry):
        offset, fraction = shear_of(p)
        roll_a = lax.rem(LANES - offset, LANES)
        roll_b = LANES - 1 - offset
        mask_a = lane < LANES - offset
        mask_b = lane < LANES - 1 - offset
        for h in range(halves):
            rows = slice(SUB + SUB * h, 2 * SUB + SUB * h)
            before = [(zero, zero)] * 4
            for t in reversed(range(tiles)):
                centre = field[p + 1, t, rows, :]
                right = field[p + 1, t + 1, rows, :] if t < tiles - 1 else zero
                left = field[p + 1, t - 1, rows, :] if t > 0 else zero
                up = jnp.where(lane < LANES - 1, pltpu.roll(centre, LANES - 1, 1), pltpu.roll(right, LANES - 1, 1))
                down = jnp.where(lane > 0, pltpu.roll(centre, 1, 1), pltpu.roll(left, 1, 1))
                slope = 0.5 * (up - down)
                part_a[h, p, t] = LIGHT_X * slope
                part_q[h, p, t] = 1.0 + slope * slope
                spot = bins_v[p, SUB * h : SUB * h + SUB, t * LANES : (t + 1) * LANES]
                looked = [
                    jnp.take_along_axis(column, spot, axis=1, mode="promise_in_bounds")
                    for column in columns
                ]
                extinction = looked[0] * (1.0 + centre * centre) * (1.0 / (planes * bricks))
                opacity = 1.0 - jnp.exp(-extinction)
                fields = [extinction] + [entry * opacity for entry in looked[1:]]
                rolled = [(pltpu.roll(v, roll_a, 1), pltpu.roll(v, roll_b, 1)) for v in fields]
                first = [jnp.where(mask_a, rolled[i][0], before[i][0]) for i in range(4)]
                second = [jnp.where(mask_b, rolled[i][1], before[i][1]) for i in range(4)]
                before = rolled
                sofar = depth[h, t]
                through = jnp.exp(-sofar)
                depth[h, t] = sofar + ((1.0 - fraction) * first[0] + fraction * second[0])
                scale_a = (1.0 - fraction) * through
                scale_b = fraction * through
                for c in range(3):
                    near[c, h, p, t] = scale_a * first[c + 1]
                    far[c, h, p, t] = scale_b * second[c + 1]
        return carry

    lax.fori_loop(0, planes, plane_terms, 0)

    has_below = me > 0
    has_over = me < bricks - 1
    has_upper = strip > 0
    has_lower = strip < strips - 1
    greeted = bricks - 1 + has_upper.astype(jnp.int32) + has_lower.astype(jnp.int32)
    pl.semaphore_wait(barrier, greeted)

    def halo(src, dst, slot, target):
        return pltpu.make_async_remote_copy(
            src_ref=src, dst_ref=dst, send_sem=halo_send.at[slot], recv_sem=halo_recv.at[slot],
            device_id=target, device_id_type=MESH,
        )

    to_over = halo(dens_v.at[planes - 1], plane_in.at[0], 0, {"depth": lax.rem(me + 1, bricks)})
    to_below = halo(dens_v.at[0], plane_in.at[1], 1, {"depth": lax.rem(me + bricks - 1, bricks)})
    to_lower = halo(rows_out.at[1], rows_in.at[0], 2, {"strip": lax.rem(strip + 1, strips)})
    to_upper = halo(rows_out.at[0], rows_in.at[1], 3, {"strip": lax.rem(strip + strips - 1, strips)})

    pl.when(has_over)(to_over.start)
    pl.when(has_below)(to_below.start)
    pl.when(has_lower)(to_lower.start)
    pl.when(has_upper)(to_upper.start)

    @pl.when(has_below)
    def _():
        to_over.wait_recv()
        for t in range(tiles):
            field[0, t, SUB : SUB + height, :] = plane_in[0, :, t * LANES : (t + 1) * LANES].astype(F32)

    @pl.when(jnp.logical_not(has_below))
    def _():
        for t in range(tiles):
            field[0, t, SUB : SUB + height, :] = jnp.zeros((height, LANES), F32)

    @pl.when(has_over)
    def _():
        to_below.wait_recv()
        for t in range(tiles):
            field[planes + 1, t, SUB : SUB + height, :] = plane_in[1, :, t * LANES : (t + 1) * LANES].astype(F32)

    @pl.when(jnp.logical_not(has_over))
    def _():
        for t in range(tiles):
            field[planes + 1, t, SUB : SUB + height, :] = jnp.zeros((height, LANES), F32)

    @pl.when(has_upper)
    def _():
        to_lower.wait_recv()
        for p in range(planes):
            for t in range(tiles):
                field[p + 1, t, SUB - 1 : SUB, :] = rows_in[0, p, t : t + 1, :]

    @pl.when(jnp.logical_not(has_upper))
    def _():
        for p in range(planes):
            for t in range(tiles):
                field[p + 1, t, SUB - 1 : SUB, :] = jnp.zeros((1, LANES), F32)

    @pl.when(has_lower)
    def _():
        to_upper.wait_recv()
        for p in range(planes):
            for t in range(tiles):
                field[p + 1, t, SUB + height : SUB + height + 1, :] = rows_in[1, p, t : t + 1, :]

    @pl.when(jnp.logical_not(has_lower))
    def _():
        for p in range(planes):
            for t in range(tiles):
                field[p + 1, t, SUB + height : SUB + height + 1, :] = jnp.zeros((1, LANES), F32)

    def tile_copy(owner):
        return pltpu.make_async_remote_copy(
            src_ref=packed.at[owner], dst_ref=arrived.at[me], send_sem=tile_send, recv_sem=tile_recv,
            device_id={"depth": owner}, device_id_type=MESH,
        )

    shears = [shear_of(p) for p in range(planes)]
    owners = bricks // halves
    for h in range(halves):
        rows = slice(SUB + SUB * h, 2 * SUB + SUB * h)
        above = slice(SUB + SUB * h - 1, 2 * SUB + SUB * h - 1)
        under = slice(SUB + SUB * h + 1, 2 * SUB + SUB * h + 1)
        before = [(zero, zero)] * planes
        for t in reversed(range(tiles)):
            colour = [zero] * 3
            for p in range(planes):
                offset = shears[p][0]
                slope_down = 0.5 * (field[p + 1, t, under, :] - field[p + 1, t, above, :])
                slope_deep = 0.5 * (field[p + 2, t, rows, :] - field[p, t, rows, :])
                square = part_q[h, p, t] + slope_down * slope_down + slope_deep * slope_deep
                toward = part_a[h, p, t] + LIGHT_Y * slope_down + LIGHT_Z * slope_deep
                gain = jnp.exp(SHADE_GAIN * toward * lax.rsqrt(square))
                gain_a = pltpu.roll(gain, lax.rem(LANES - offset, LANES), 1)
                gain_b = pltpu.roll(gain, LANES - 1 - offset, 1)
                first = jnp.where(lane < LANES - offset, gain_a, before[p][0])
                second = jnp.where(lane < LANES - 1 - offset, gain_b, before[p][1])
                before[p] = (gain_a, gain_b)
                for c in range(3):
                    colour[c] = colour[c] + (near[c, h, p, t] * first + far[c, h, p, t] * second)
            spot = SUB * h * tiles + t
            start = spot // per_owner * rows_msg + spot % per_owner
            for c, value in enumerate(colour + [depth[h, t]]):
                wide[pl.ds(start + c * per_owner, SUB, stride=tiles * 4), :] = value
        for owner in range(owners * h, owners * (h + 1)):
            packed[owner] = wide[owner * rows_msg : (owner + 1) * rows_msg, :].astype(jnp.bfloat16)

        def send(step, carry, h=h):
            owner = owners * h + lax.rem(me + step, owners)
            pl.when(owner != me)(lambda: tile_copy(owner).start())
            return carry

        lax.fori_loop(0, owners, send, 0)

    arrived[me] = packed[me]
    loads[3].wait()
    pl.when(has_over)(to_over.wait_send)
    pl.when(has_below)(to_below.wait_send)
    pl.when(has_lower)(to_lower.wait_send)
    pl.when(has_upper)(to_upper.wait_send)
    everyone = pltpu.make_async_remote_copy(
        src_ref=packed.at[pl.ds(0, bricks - 1)], dst_ref=arrived.at[pl.ds(0, bricks - 1)],
        send_sem=tile_send, recv_sem=tile_recv,
        device_id={"depth": lax.rem(me + 1, bricks)}, device_id_type=MESH,
    )
    everyone.wait_recv()

    row = lax.broadcasted_iota(jnp.int32, (rows_msg, LANES), 0)
    last = row >= 3 * per_owner

    def layer(slot, carry):
        shown, prefix = carry
        for inner in range(8):
            tile = arrived[order_s[0, slot * 8 + inner]].astype(F32)
            shown = shown + jnp.exp(-prefix) * tile
            spread = jnp.where(last, tile, 0.0)
            spread = spread + pltpu.roll(spread, 2 * per_owner, 0)
            spread = spread + pltpu.roll(spread, per_owner, 0)
            prefix = prefix + spread
        return shown, prefix

    blank = jnp.zeros((rows_msg, LANES), F32)
    shown, prefix = lax.fori_loop(0, bricks // 8, layer, (blank, blank))
    shown = jnp.where(last, jnp.exp(-prefix), shown)
    for r in range(rows_msg):
        c, piece = r // per_owner, r % per_owner
        out_ref[c : c + 1, piece * LANES : (piece + 1) * LANES] = shown[r : r + 1, :]
    everyone.wait_send()


def solution(mesh):
    bricks = mesh.shape["depth"]
    strips = mesh.shape["strip"]

    def per_device(density, tf_bins, tf_table, brick_order):
        planes, height, across = density.shape
        classes = tf_table.shape[1]
        tiles = across // LANES
        halves = height // SUB
        owned = height * across // bricks
        rows_msg = 4 * owned // LANES
        return pl.pallas_call(
            functools.partial(kernel, bricks, strips, planes, height, across, classes),
            out_shape=jax.ShapeDtypeStruct((4, owned), F32),
            in_specs=[pl.BlockSpec(memory_space=pl.ANY)] * 4,
            out_specs=pl.BlockSpec(memory_space=pltpu.VMEM),
            scratch_shapes=[
                pltpu.VMEM((planes, height, across), jnp.bfloat16),
                pltpu.VMEM((planes, height, across), jnp.int32),
                pltpu.VMEM((4, classes), F32),
                pltpu.SMEM((1, bricks), jnp.int32),
                pltpu.VMEM((SUB, LANES), F32),
                pltpu.VMEM((planes + 2, tiles, height + 2 * SUB, LANES), F32),
                pltpu.VMEM((2, planes, tiles, LANES), F32),
                pltpu.VMEM((2, planes, tiles, LANES), F32),
                pltpu.VMEM((2, height, across), jnp.bfloat16),
                pltpu.VMEM((halves, planes, tiles, SUB, LANES), F32),
                pltpu.VMEM((halves, planes, tiles, SUB, LANES), F32),
                pltpu.VMEM((3, halves, planes, tiles, SUB, LANES), F32),
                pltpu.VMEM((3, halves, planes, tiles, SUB, LANES), F32),
                pltpu.VMEM((halves, tiles, SUB, LANES), F32),
                pltpu.VMEM((bricks * rows_msg, LANES), F32),
                pltpu.VMEM((bricks, rows_msg, LANES), jnp.bfloat16),
                pltpu.VMEM((bricks, rows_msg, LANES), jnp.bfloat16),
                pltpu.SemaphoreType.DMA((4,)),
                pltpu.SemaphoreType.DMA((4,)),
                pltpu.SemaphoreType.DMA((4,)),
                pltpu.SemaphoreType.DMA,
                pltpu.SemaphoreType.DMA,
            ],
            compiler_params=pltpu.CompilerParams(collective_id=0, has_side_effects=True),
        )(density, tf_bins, tf_table, brick_order)

    return jax.shard_map(
        per_device,
        mesh=mesh,
        in_specs=(P("depth", "strip", None), P("depth", "strip", None), P(), P("strip", None)),
        out_specs=P(None, ("strip", "depth")),
        check_vma=False,
    )
```

```python
import functools

import jax
import jax.numpy as jnp
from jax import lax
from jax.experimental import pallas as pl
from jax.experimental.pallas import tpu as pltpu
from jax.sharding import PartitionSpec as P

LIGHT_X = 0.36
LIGHT_Y = 0.48
LIGHT_Z = 0.8
SHADE_GAIN = 1.5
MESH = pl.DeviceIdType.MESH
LANES = 128
RING = 8
SUB = 8
F32 = jnp.float32


def kernel(
    bricks, strips, planes, height, across, classes,
    dens_hbm, bins_hbm, table_hbm, order_hbm, out_ref,
    dens_v, bins_v, table_v, order_s, tab, field, rows_out, rows_in, plane_in,
    raw, part_a, part_q, near, far, depth, wide, packed, arrived,
    in_sem, halo_send, halo_recv, tile_send, tile_recv, late_in, all_in,
):
    me = lax.axis_index("depth")
    strip = lax.axis_index("strip")
    tiles = across // LANES
    halves = height // SUB
    per_owner = height * tiles // bricks
    rows_msg = 4 * per_owner

    cores = 2
    deep = min(RING, bricks // cores)
    rows_x = bricks // (cores * deep)
    core = me % cores
    z = me // cores % deep
    x = me // (cores * deep)
    half = deep // 2
    late = z >= half
    early = jnp.logical_not(late)
    has_below = me > 0
    has_over = me < bricks - 1
    has_upper = strip > 0
    has_lower = strip < strips - 1
    below = lax.rem(me + bricks - 1, bricks)
    over = lax.rem(me + 1, bricks)

    def place(x_to, z_to, core_to):
        return (x_to * deep + z_to) * cores + core_to

    def is_late(index):
        return index // cores % deep >= half

    def signal(sem, target):
        pl.semaphore_signal(sem, inc=1, device_id=target, device_id_type=MESH)

    barrier = pltpu.get_barrier_semaphore()

    @pl.when(has_upper)
    def _():
        signal(barrier, {"strip": strip - 1})

    @pl.when(has_lower)
    def _():
        signal(barrier, {"strip": strip + 1})

    @pl.when(jnp.logical_and(late, has_below))
    def _():
        signal(barrier, {"depth": below})

    @pl.when(jnp.logical_and(late, has_over))
    def _():
        signal(barrier, {"depth": over})

    @pl.when(early)
    def _():
        def greet(step, carry):
            signal(barrier, {"depth": lax.rem(me + step, bricks)})
            return carry

        lax.fori_loop(1, bricks, greet, 0)

    greeted = (
        bricks // 2
        - early.astype(jnp.int32)
        + has_upper.astype(jnp.int32)
        + has_lower.astype(jnp.int32)
        + jnp.logical_and(has_below, is_late(below)).astype(jnp.int32)
        + jnp.logical_and(has_over, is_late(over)).astype(jnp.int32)
    )

    def halo(src, dst, slot, target):
        return pltpu.make_async_remote_copy(
            src_ref=src, dst_ref=dst, send_sem=halo_send.at[slot], recv_sem=halo_recv.at[slot],
            device_id=target, device_id_type=MESH,
        )

    to_over = halo(dens_hbm.at[planes - 1], plane_in.at[0], 0, {"depth": over})
    to_below = halo(dens_hbm.at[0], plane_in.at[1], 1, {"depth": below})
    to_lower = halo(rows_out.at[1], rows_in.at[0], 2, {"strip": lax.rem(strip + 1, strips)})
    to_upper = halo(rows_out.at[0], rows_in.at[1], 3, {"strip": lax.rem(strip + strips - 1, strips)})

    loads = [
        pltpu.make_async_copy(dens_hbm, dens_v, in_sem.at[0]),
        pltpu.make_async_copy(bins_hbm, bins_v, in_sem.at[1]),
        pltpu.make_async_copy(table_hbm, table_v, in_sem.at[2]),
        pltpu.make_async_copy(order_hbm, order_s, in_sem.at[3]),
    ]
    for load in loads:
        load.start()

    pl.semaphore_wait(barrier, greeted)
    pl.when(has_over)(to_over.start)
    pl.when(has_below)(to_below.start)

    loads[0].wait()
    for p in range(planes):
        for t in range(tiles):
            field[p + 1, t, SUB : SUB + height, :] = dens_v[
                p, :, t * LANES : (t + 1) * LANES
            ].astype(F32)
    for p in range(planes):
        for t in range(tiles):
            rows_out[0, p, t : t + 1, :] = field[p + 1, t, SUB : SUB + 1, :]
            rows_out[1, p, t : t + 1, :] = field[p + 1, t, SUB + height - 1 : SUB + height, :]
    pl.when(has_lower)(to_lower.start)
    pl.when(has_upper)(to_upper.start)

    @pl.when(late)
    def _():
        def report(step, carry):
            signal(late_in, {"depth": place(step // (half * cores), step // cores % half, step % cores)})
            return carry

        lax.fori_loop(0, bricks // 2, report, 0)

    loads[2].wait()
    tab[0:4, 0:classes] = table_v[...]
    loads[1].wait()

    lane = lax.broadcasted_iota(jnp.int32, (SUB, LANES), 1)
    zero = jnp.zeros((SUB, LANES), F32)
    columns = [jnp.broadcast_to(tab[c : c + 1, :], (SUB, LANES)) for c in range(4)]
    depth[...] = jnp.zeros_like(depth)

    def shear_of(p):
        scaled = 3 * (me * planes + p)
        offset = scaled // 8
        fraction = (scaled % 8).astype(F32) * 0.125
        return offset, fraction

    def look_up(p, carry):
        for h in range(halves):
            rows = slice(SUB + SUB * h, 2 * SUB + SUB * h)
            for t in range(tiles):
                centre = field[p + 1, t, rows, :]
                spot = bins_v[p, SUB * h : SUB * h + SUB, t * LANES : (t + 1) * LANES]
                looked = [
                    jnp.take_along_axis(column, spot, axis=1, mode="promise_in_bounds")
                    for column in columns
                ]
                extinction = looked[0] * (1.0 + centre * centre) * (1.0 / (planes * bricks))
                opacity = 1.0 - jnp.exp(-extinction)
                raw[0, h, p, t] = extinction
                for c in range(3):
                    raw[c + 1, h, p, t] = looked[c + 1] * opacity
        return carry

    lax.fori_loop(0, planes, look_up, 0)

    def plane_terms(p, carry):
        offset, fraction = shear_of(p)
        roll_a = lax.rem(LANES - offset, LANES)
        roll_b = LANES - 1 - offset
        mask_a = lane < LANES - offset
        mask_b = lane < LANES - 1 - offset
        for h in range(halves):
            rows = slice(SUB + SUB * h, 2 * SUB + SUB * h)
            before = [(zero, zero)] * 4
            for t in reversed(range(tiles)):
                centre = field[p + 1, t, rows, :]
                right = field[p + 1, t + 1, rows, :] if t < tiles - 1 else zero
                left = field[p + 1, t - 1, rows, :] if t > 0 else zero
                up = jnp.where(lane < LANES - 1, pltpu.roll(centre, LANES - 1, 1), pltpu.roll(right, LANES - 1, 1))
                down = jnp.where(lane > 0, pltpu.roll(centre, 1, 1), pltpu.roll(left, 1, 1))
                slope = 0.5 * (up - down)
                part_a[h, p, t] = LIGHT_X * slope
                part_q[h, p, t] = 1.0 + slope * slope
                fields = [raw[c, h, p, t] for c in range(4)]
                rolled = [(pltpu.roll(v, roll_a, 1), pltpu.roll(v, roll_b, 1)) for v in fields]
                first = [jnp.where(mask_a, rolled[i][0], before[i][0]) for i in range(4)]
                second = [jnp.where(mask_b, rolled[i][1], before[i][1]) for i in range(4)]
                before = rolled
                sofar = depth[h, t]
                through = jnp.exp(-sofar)
                depth[h, t] = sofar + ((1.0 - fraction) * first[0] + fraction * second[0])
                scale_a = (1.0 - fraction) * through
                scale_b = fraction * through
                for c in range(3):
                    near[c, h, p, t] = scale_a * first[c + 1]
                    far[c, h, p, t] = scale_b * second[c + 1]
        return carry

    lax.fori_loop(0, planes, plane_terms, 0)

    @pl.when(has_below)
    def _():
        to_over.wait_recv()
        for t in range(tiles):
            field[0, t, SUB : SUB + height, :] = plane_in[0, :, t * LANES : (t + 1) * LANES].astype(F32)

    @pl.when(jnp.logical_not(has_below))
    def _():
        for t in range(tiles):
            field[0, t, SUB : SUB + height, :] = jnp.zeros((height, LANES), F32)

    @pl.when(has_over)
    def _():
        to_below.wait_recv()
        for t in range(tiles):
            field[planes + 1, t, SUB : SUB + height, :] = plane_in[1, :, t * LANES : (t + 1) * LANES].astype(F32)

    @pl.when(jnp.logical_not(has_over))
    def _():
        for t in range(tiles):
            field[planes + 1, t, SUB : SUB + height, :] = jnp.zeros((height, LANES), F32)

    @pl.when(has_upper)
    def _():
        to_lower.wait_recv()
        for p in range(planes):
            for t in range(tiles):
                field[p + 1, t, SUB - 1 : SUB, :] = rows_in[0, p, t : t + 1, :]

    @pl.when(jnp.logical_not(has_upper))
    def _():
        for p in range(planes):
            for t in range(tiles):
                field[p + 1, t, SUB - 1 : SUB, :] = jnp.zeros((1, LANES), F32)

    @pl.when(has_lower)
    def _():
        to_upper.wait_recv()
        for p in range(planes):
            for t in range(tiles):
                field[p + 1, t, SUB + height : SUB + height + 1, :] = rows_in[1, p, t : t + 1, :]

    @pl.when(jnp.logical_not(has_lower))
    def _():
        for p in range(planes):
            for t in range(tiles):
                field[p + 1, t, SUB + height : SUB + height + 1, :] = jnp.zeros((1, LANES), F32)

    def tile_copy(owner):
        return pltpu.make_async_remote_copy(
            src_ref=packed.at[owner], dst_ref=arrived.at[me], send_sem=tile_send, recv_sem=tile_recv,
            device_id={"depth": owner}, device_id_type=MESH,
        )

    def send(z_to, carry):
        for step in range(rows_x):
            for core_to in range(cores):
                owner = place(lax.rem(x + step, rows_x), z_to, core_to)
                if step == 0:
                    pl.when(owner != me)(lambda owner=owner: tile_copy(owner).start())
                else:
                    tile_copy(owner).start()
        return carry

    shears = [shear_of(p) for p in range(planes)]
    for h in range(halves):
        rows = slice(SUB + SUB * h, 2 * SUB + SUB * h)
        above = slice(SUB + SUB * h - 1, 2 * SUB + SUB * h - 1)
        under = slice(SUB + SUB * h + 1, 2 * SUB + SUB * h + 1)
        before = [(zero, zero)] * planes
        for t in reversed(range(tiles)):
            colour = [zero] * 3
            for p in range(planes):
                offset = shears[p][0]
                slope_down = 0.5 * (field[p + 1, t, under, :] - field[p + 1, t, above, :])
                slope_deep = 0.5 * (field[p + 2, t, rows, :] - field[p, t, rows, :])
                square = part_q[h, p, t] + slope_down * slope_down + slope_deep * slope_deep
                toward = part_a[h, p, t] + LIGHT_Y * slope_down + LIGHT_Z * slope_deep
                gain = jnp.exp(SHADE_GAIN * toward * lax.rsqrt(square))
                gain_a = pltpu.roll(gain, lax.rem(LANES - offset, LANES), 1)
                gain_b = pltpu.roll(gain, LANES - 1 - offset, 1)
                first = jnp.where(lane < LANES - offset, gain_a, before[p][0])
                second = jnp.where(lane < LANES - 1 - offset, gain_b, before[p][1])
                before[p] = (gain_a, gain_b)
                for c in range(3):
                    colour[c] = colour[c] + (near[c, h, p, t] * first + far[c, h, p, t] * second)
            spot = SUB * h * tiles + t
            start = spot // per_owner * rows_msg + spot % per_owner
            for c, value in enumerate(colour + [depth[h, t]]):
                wide[pl.ds(start + c * per_owner, SUB, stride=tiles * 4), :] = value

    for owner in range(bricks):
        packed[owner] = wide[owner * rows_msg : (owner + 1) * rows_msg, :].astype(jnp.bfloat16)

    lax.fori_loop(0, half, send, 0)

    @pl.when(early)
    def _():
        pl.semaphore_wait(late_in, bricks // 2)

        @pl.when(z == 0)
        def _():
            signal(all_in, {"depth": place(x, deep - 1, core)})
            signal(all_in, {"depth": place(x, deep - 2, core)})

        @pl.when(z == half - 1)
        def _():
            signal(all_in, {"depth": place(x, half, core)})
            signal(all_in, {"depth": place(x, half + 1, core)})

    @pl.when(late)
    def _():
        pl.semaphore_wait(all_in, 1)

    lax.fori_loop(half, deep, send, 0)

    arrived[me] = packed[me]
    loads[3].wait()
    pl.when(has_over)(to_over.wait_send)
    pl.when(has_below)(to_below.wait_send)
    pl.when(has_lower)(to_lower.wait_send)
    pl.when(has_upper)(to_upper.wait_send)
    everyone = pltpu.make_async_remote_copy(
        src_ref=packed.at[pl.ds(0, bricks - 1)], dst_ref=arrived.at[pl.ds(0, bricks - 1)],
        send_sem=tile_send, recv_sem=tile_recv,
        device_id={"depth": lax.rem(me + 1, bricks)}, device_id_type=MESH,
    )
    everyone.wait_recv()

    row = lax.broadcasted_iota(jnp.int32, (rows_msg, LANES), 0)
    last = row >= 3 * per_owner

    def layer(slot, carry):
        shown, prefix = carry
        for inner in range(8):
            tile = arrived[order_s[0, slot * 8 + inner]].astype(F32)
            shown = shown + jnp.exp(-prefix) * tile
            spread = jnp.where(last, tile, 0.0)
            spread = spread + pltpu.roll(spread, 2 * per_owner, 0)
            spread = spread + pltpu.roll(spread, per_owner, 0)
            prefix = prefix + spread
        return shown, prefix

    blank = jnp.zeros((rows_msg, LANES), F32)
    shown, prefix = lax.fori_loop(0, bricks // 8, layer, (blank, blank))
    shown = jnp.where(last, jnp.exp(-prefix), shown)
    for r in range(rows_msg):
        c, piece = r // per_owner, r % per_owner
        out_ref[c : c + 1, piece * LANES : (piece + 1) * LANES] = shown[r : r + 1, :]
    everyone.wait_send()


def solution(mesh):
    bricks = mesh.shape["depth"]
    strips = mesh.shape["strip"]

    def per_device(density, tf_bins, tf_table, brick_order):
        planes, height, across = density.shape
        classes = tf_table.shape[1]
        tiles = across // LANES
        halves = height // SUB
        owned = height * across // bricks
        rows_msg = 4 * owned // LANES
        return pl.pallas_call(
            functools.partial(kernel, bricks, strips, planes, height, across, classes),
            out_shape=jax.ShapeDtypeStruct((4, owned), F32),
            in_specs=[pl.BlockSpec(memory_space=pl.ANY)] * 4,
            out_specs=pl.BlockSpec(memory_space=pltpu.VMEM),
            scratch_shapes=[
                pltpu.VMEM((planes, height, across), jnp.bfloat16),
                pltpu.VMEM((planes, height, across), jnp.int32),
                pltpu.VMEM((4, classes), F32),
                pltpu.SMEM((1, bricks), jnp.int32),
                pltpu.VMEM((SUB, LANES), F32),
                pltpu.VMEM((planes + 2, tiles, height + 2 * SUB, LANES), F32),
                pltpu.VMEM((2, planes, tiles, LANES), F32),
                pltpu.VMEM((2, planes, tiles, LANES), F32),
                pltpu.VMEM((2, height, across), jnp.bfloat16),
                pltpu.VMEM((4, halves, planes, tiles, SUB, LANES), F32),
                pltpu.VMEM((halves, planes, tiles, SUB, LANES), F32),
                pltpu.VMEM((halves, planes, tiles, SUB, LANES), F32),
                pltpu.VMEM((3, halves, planes, tiles, SUB, LANES), F32),
                pltpu.VMEM((3, halves, planes, tiles, SUB, LANES), F32),
                pltpu.VMEM((halves, tiles, SUB, LANES), F32),
                pltpu.VMEM((bricks * rows_msg, LANES), F32),
                pltpu.VMEM((bricks, rows_msg, LANES), jnp.bfloat16),
                pltpu.VMEM((bricks, rows_msg, LANES), jnp.bfloat16),
                pltpu.SemaphoreType.DMA((4,)),
                pltpu.SemaphoreType.DMA((4,)),
                pltpu.SemaphoreType.DMA((4,)),
                pltpu.SemaphoreType.DMA,
                pltpu.SemaphoreType.DMA,
                pltpu.SemaphoreType.REGULAR,
                pltpu.SemaphoreType.REGULAR,
            ],
            compiler_params=pltpu.CompilerParams(collective_id=0, has_side_effects=True),
        )(density, tf_bins, tf_table, brick_order)

    return jax.shard_map(
        per_device,
        mesh=mesh,
        in_specs=(P("depth", "strip", None), P("depth", "strip", None), P(), P("strip", None)),
        out_specs=P(None, ("strip", "depth")),
        check_vma=False,
    )
```

```python
import functools

import jax
import jax.numpy as jnp
from jax import lax
from jax.experimental import pallas as pl
from jax.experimental.pallas import tpu as pltpu
from jax.sharding import PartitionSpec as P

LIGHT_X = 0.36
LIGHT_Y = 0.48
LIGHT_Z = 0.8
SHADE_GAIN = 1.5
MESH = pl.DeviceIdType.MESH
LANES = 128
RING = 8
EARLY = 3
RELAYS = ((0, (7, 6)), (2, (3, 4, 5)))
SUB = 8
F32 = jnp.float32


def kernel(
    bricks, strips, planes, height, across, classes,
    dens_hbm, bins_hbm, table_hbm, arrived,
    dens_v, bins_v, table_v, tab, field, rows_out, rows_in, plane_in,
    raw, part_a, part_q, near, far, depth, wide, packed,
    in_sem, own_sem, halo_send, halo_recv, tile_send, tile_recv, late_in, all_in,
):
    me = lax.axis_index("depth")
    strip = lax.axis_index("strip")
    tiles = across // LANES
    halves = height // SUB
    per_owner = height * tiles // bricks
    rows_msg = 4 * per_owner

    cores = 2
    deep = min(RING, bricks // cores)
    rows_x = bricks // (cores * deep)
    core = me % cores
    z = me // cores % deep
    x = me // (cores * deep)
    late = z >= EARLY
    pitch = height + 2 * SUB
    early = jnp.logical_not(late)
    has_below = me > 0
    has_over = me < bricks - 1
    has_upper = strip > 0
    has_lower = strip < strips - 1
    below = lax.rem(me + bricks - 1, bricks)
    over = lax.rem(me + 1, bricks)

    def place(x_to, z_to, core_to):
        return (x_to * deep + z_to) * cores + core_to

    def is_late(index):
        return index // cores % deep >= EARLY

    def signal(sem, target):
        pl.semaphore_signal(sem, inc=1, device_id=target, device_id_type=MESH)

    def at(p, t, row, count=SUB):
        start = (p * tiles + t) * pitch + SUB + row
        if not isinstance(start, int) and row % SUB == 0:
            start = pl.multiple_of(start, SUB)
        return pl.ds(start, count)

    def put(p, t, value):
        field[at(p, t, 0, height), :] = value

    def row_of(p, row):
        return pl.ds(p * tiles * pitch + SUB + row, tiles, stride=pitch)

    barrier = pltpu.get_barrier_semaphore()

    @pl.when(has_upper)
    def _():
        signal(barrier, {"strip": strip - 1})

    @pl.when(has_lower)
    def _():
        signal(barrier, {"strip": strip + 1})

    @pl.when(jnp.logical_and(late, has_below))
    def _():
        signal(barrier, {"depth": below})

    @pl.when(jnp.logical_and(late, has_over))
    def _():
        signal(barrier, {"depth": over})

    @pl.when(early)
    def _():
        def greet(step, carry):
            signal(barrier, {"depth": lax.rem(me + step, bricks)})
            return carry

        lax.fori_loop(1, bricks, greet, 0)

    greeted = (
        EARLY * rows_x * cores
        - early.astype(jnp.int32)
        + has_upper.astype(jnp.int32)
        + has_lower.astype(jnp.int32)
        + jnp.logical_and(has_below, is_late(below)).astype(jnp.int32)
        + jnp.logical_and(has_over, is_late(over)).astype(jnp.int32)
    )

    def halo(src, dst, slot, target):
        return pltpu.make_async_remote_copy(
            src_ref=src, dst_ref=dst, send_sem=halo_send.at[slot], recv_sem=halo_recv.at[slot],
            device_id=target, device_id_type=MESH,
        )

    to_over = halo(dens_hbm.at[planes - 1], plane_in.at[0], 0, {"depth": over})
    to_below = halo(dens_hbm.at[0], plane_in.at[1], 1, {"depth": below})
    to_lower = halo(rows_out.at[1], rows_in.at[0], 2, {"strip": lax.rem(strip + 1, strips)})
    to_upper = halo(rows_out.at[0], rows_in.at[1], 3, {"strip": lax.rem(strip + strips - 1, strips)})

    loads = [
        pltpu.make_async_copy(dens_hbm, dens_v, in_sem.at[0]),
        pltpu.make_async_copy(bins_hbm, bins_v, in_sem.at[1]),
        pltpu.make_async_copy(table_hbm, table_v, in_sem.at[2]),
    ]
    for load in loads:
        load.start()

    pl.semaphore_wait(barrier, greeted)
    pl.when(has_over)(to_over.start)
    pl.when(has_below)(to_below.start)

    loads[0].wait()
    for p in range(planes):
        for t in range(tiles):
            put(p + 1, t, dens_v[p, :, t * LANES : (t + 1) * LANES].astype(F32))
    for p in range(planes):
        rows_out[0, p] = field[row_of(p + 1, 0), :].astype(jnp.bfloat16)
        rows_out[1, p] = field[row_of(p + 1, height - 1), :].astype(jnp.bfloat16)
    pl.when(has_lower)(to_lower.start)
    pl.when(has_upper)(to_upper.start)

    @pl.when(late)
    def _():
        def report(step, carry):
            signal(late_in, {"depth": place(step // (EARLY * cores), step // cores % EARLY, step % cores)})
            return carry

        lax.fori_loop(0, EARLY * rows_x * cores, report, 0)

    loads[2].wait()
    tab[0:4, 0:classes] = table_v[...]
    loads[1].wait()

    lane = lax.broadcasted_iota(jnp.int32, (SUB, LANES), 1)
    zero = jnp.zeros((SUB, LANES), F32)
    columns = [jnp.broadcast_to(tab[c : c + 1, :], (SUB, LANES)) for c in range(4)]
    depth[...] = jnp.zeros_like(depth)

    def shear_of(p):
        scaled = 3 * (me * planes + p)
        offset = scaled // 8
        fraction = (scaled % 8).astype(F32) * 0.125
        return offset, fraction

    def look_up(p, carry):
        for h in range(halves):
            for t in range(tiles):
                centre = field[at(p + 1, t, SUB * h), :]
                spot = bins_v[p, SUB * h : SUB * h + SUB, t * LANES : (t + 1) * LANES]
                looked = [
                    jnp.take_along_axis(column, spot, axis=1, mode="promise_in_bounds")
                    for column in columns
                ]
                extinction = looked[0] * (1.0 + centre * centre) * (1.0 / (planes * bricks))
                opacity = 1.0 - jnp.exp(-extinction)
                raw[0, h, p, t] = extinction
                for c in range(3):
                    raw[c + 1, h, p, t] = looked[c + 1] * opacity
        return carry

    lax.fori_loop(0, planes, look_up, 0)

    def plane_terms(p, carry):
        offset, fraction = shear_of(p)
        roll_a = lax.rem(LANES - offset, LANES)
        roll_b = LANES - 1 - offset
        mask_a = lane < LANES - offset
        mask_b = lane < LANES - 1 - offset
        for h in range(halves):
            before = [(zero, zero)] * 4
            for t in reversed(range(tiles)):
                centre = field[at(p + 1, t, SUB * h), :]
                right = field[at(p + 1, t + 1, SUB * h), :] if t < tiles - 1 else zero
                left = field[at(p + 1, t - 1, SUB * h), :] if t > 0 else zero
                up = jnp.where(lane < LANES - 1, pltpu.roll(centre, LANES - 1, 1), pltpu.roll(right, LANES - 1, 1))
                down = jnp.where(lane > 0, pltpu.roll(centre, 1, 1), pltpu.roll(left, 1, 1))
                slope = 0.5 * (up - down)
                part_a[h, p, t] = LIGHT_X * slope
                part_q[h, p, t] = 1.0 + slope * slope
                fields = [raw[c, h, p, t] for c in range(4)]
                rolled = [(pltpu.roll(v, roll_a, 1), pltpu.roll(v, roll_b, 1)) for v in fields]
                first = [jnp.where(mask_a, rolled[i][0], before[i][0]) for i in range(4)]
                second = [jnp.where(mask_b, rolled[i][1], before[i][1]) for i in range(4)]
                before = rolled
                sofar = depth[h, t]
                through = jnp.exp(-sofar)
                depth[h, t] = sofar + ((1.0 - fraction) * first[0] + fraction * second[0])
                scale_a = (1.0 - fraction) * through
                scale_b = fraction * through
                for c in range(3):
                    near[c, h, p, t] = scale_a * first[c + 1]
                    far[c, h, p, t] = scale_b * second[c + 1]
        return carry

    lax.fori_loop(0, planes, plane_terms, 0)

    def fill(present, copy, slot, p):
        @pl.when(present)
        def _():
            copy.wait_recv()
            for t in range(tiles):
                put(p, t, plane_in[slot, :, t * LANES : (t + 1) * LANES].astype(F32))

        @pl.when(jnp.logical_not(present))
        def _():
            for t in range(tiles):
                put(p, t, jnp.zeros((height, LANES), F32))

    fill(has_below, to_over, 0, 0)
    fill(has_over, to_below, 1, planes + 1)

    def border(present, copy, slot, row):
        @pl.when(present)
        def _():
            copy.wait_recv()
            for p in range(planes):
                field[row_of(p + 1, row), :] = rows_in[slot, p].astype(F32)

        @pl.when(jnp.logical_not(present))
        def _():
            for p in range(planes):
                field[row_of(p + 1, row), :] = jnp.zeros((tiles, LANES), F32)

    border(has_upper, to_lower, 0, -1)
    border(has_lower, to_upper, 1, height)

    def tile_copy(owner):
        return pltpu.make_async_remote_copy(
            src_ref=packed.at[owner], dst_ref=arrived.at[me], send_sem=tile_send, recv_sem=tile_recv,
            device_id={"depth": owner}, device_id_type=MESH,
        )

    def send(z_to, carry):
        for step in range(rows_x):
            for core_to in range(cores):
                owner = place(lax.rem(x + step, rows_x), z_to, core_to)
                if step == 0:
                    pl.when(owner != me)(lambda owner=owner: tile_copy(owner).start())
                else:
                    tile_copy(owner).start()
        return carry

    shears = [shear_of(p) for p in range(planes)]
    split = tiles // 2 if 4 * per_owner == tiles else 0

    def shade(low, high):
        for h in range(halves):
            before = [(zero, zero)] * planes
            for t in reversed(range(low, min(high + 1, tiles))):
                colour = [zero] * 3
                for p in range(planes):
                    offset = shears[p][0]
                    row = SUB * h
                    slope_down = 0.5 * (field[at(p + 1, t, row + 1), :] - field[at(p + 1, t, row - 1), :])
                    slope_deep = 0.5 * (field[at(p + 2, t, row), :] - field[at(p, t, row), :])
                    square = part_q[h, p, t] + slope_down * slope_down + slope_deep * slope_deep
                    toward = part_a[h, p, t] + LIGHT_Y * slope_down + LIGHT_Z * slope_deep
                    gain = jnp.exp(SHADE_GAIN * toward * lax.rsqrt(square))
                    gain_a = pltpu.roll(gain, lax.rem(LANES - offset, LANES), 1)
                    gain_b = pltpu.roll(gain, LANES - 1 - offset, 1)
                    if t < high:
                        first = jnp.where(lane < LANES - offset, gain_a, before[p][0])
                        second = jnp.where(lane < LANES - 1 - offset, gain_b, before[p][1])
                        for c in range(3):
                            colour[c] = colour[c] + (near[c, h, p, t] * first + far[c, h, p, t] * second)
                    before[p] = (gain_a, gain_b)
                if t < high:
                    spot = SUB * h * tiles + t
                    start = spot // per_owner * rows_msg + spot % per_owner
                    for c, value in enumerate(colour + [depth[h, t]]):
                        wide[pl.ds(start + c * per_owner, SUB, stride=tiles * 4), :] = value
        for owner in range(bricks):
            first_tile = owner * per_owner % tiles
            if low <= first_tile < high:
                packed[owner] = wide[owner * rows_msg : (owner + 1) * rows_msg, :].astype(jnp.bfloat16)

    if split:
        shade(0, split)
        send(0, 0)
        shade(split, tiles)
    else:
        shade(0, tiles)
        send(0, 0)
    lax.fori_loop(1, EARLY, send, 0)

    @pl.when(early)
    def _():
        pl.semaphore_wait(late_in, (deep - EARLY) * rows_x * cores)
        for source, targets in RELAYS:

            @pl.when(z == source)
            def _(targets=targets):
                for target in targets:
                    signal(all_in, {"depth": place(x, target, core)})

    @pl.when(late)
    def _():
        pl.semaphore_wait(all_in, 1)

    lax.fori_loop(EARLY, deep, send, 0)

    own = pltpu.make_async_copy(packed.at[me], arrived.at[me], own_sem)
    own.start()
    own.wait()
    pl.when(has_over)(to_over.wait_send)
    pl.when(has_below)(to_below.wait_send)
    pl.when(has_lower)(to_lower.wait_send)
    pl.when(has_upper)(to_upper.wait_send)
    everyone = pltpu.make_async_remote_copy(
        src_ref=packed.at[pl.ds(0, bricks - 1)], dst_ref=arrived.at[pl.ds(0, bricks - 1)],
        send_sem=tile_send, recv_sem=tile_recv,
        device_id={"depth": lax.rem(me + 1, bricks)}, device_id_type=MESH,
    )
    everyone.wait_recv()

    everyone.wait_send()


def composite(bricks, per_owner, order, arrived, out_ref):
    rows_msg = 4 * per_owner
    row = lax.broadcasted_iota(jnp.int32, (rows_msg, LANES), 0)
    last = row >= 3 * per_owner

    def layer(slot, carry):
        shown, prefix = carry
        for inner in range(8):
            tile = arrived[order[0, slot * 8 + inner]].astype(F32)
            shown = shown + jnp.exp(-prefix) * tile
            spread = jnp.where(last, tile, 0.0)
            spread = spread + pltpu.roll(spread, 2 * per_owner, 0)
            spread = spread + pltpu.roll(spread, per_owner, 0)
            prefix = prefix + spread
        return shown, prefix

    blank = jnp.zeros((rows_msg, LANES), F32)
    shown, prefix = lax.fori_loop(0, bricks // 8, layer, (blank, blank))
    shown = jnp.where(last, jnp.exp(-prefix), shown)
    for r in range(rows_msg):
        c, piece = r // per_owner, r % per_owner
        out_ref[c : c + 1, piece * LANES : (piece + 1) * LANES] = shown[r : r + 1, :]


def solution(mesh):
    bricks = mesh.shape["depth"]
    strips = mesh.shape["strip"]

    def per_device(density, tf_bins, tf_table, brick_order):
        planes, height, across = density.shape
        classes = tf_table.shape[1]
        tiles = across // LANES
        halves = height // SUB
        owned = height * across // bricks
        rows_msg = 4 * owned // LANES
        arrived = pl.pallas_call(
            functools.partial(kernel, bricks, strips, planes, height, across, classes),
            out_shape=jax.ShapeDtypeStruct((bricks, rows_msg, LANES), jnp.bfloat16),
            in_specs=[pl.BlockSpec(memory_space=pl.ANY)] * 3,
            out_specs=pl.BlockSpec(memory_space=pl.ANY),
            scratch_shapes=[
                pltpu.VMEM((planes, height, across), jnp.bfloat16),
                pltpu.VMEM((planes, height, across), jnp.int32),
                pltpu.VMEM((4, classes), F32),
                pltpu.VMEM((SUB, LANES), F32),
                pltpu.VMEM(((planes + 2) * tiles * (height + 2 * SUB), LANES), F32),
                pltpu.VMEM((2, planes, tiles, LANES), jnp.bfloat16),
                pltpu.VMEM((2, planes, tiles, LANES), jnp.bfloat16),
                pltpu.VMEM((2, height, across), jnp.bfloat16),
                pltpu.VMEM((4, halves, planes, tiles, SUB, LANES), F32),
                pltpu.VMEM((halves, planes, tiles, SUB, LANES), F32),
                pltpu.VMEM((halves, planes, tiles, SUB, LANES), F32),
                pltpu.VMEM((3, halves, planes, tiles, SUB, LANES), F32),
                pltpu.VMEM((3, halves, planes, tiles, SUB, LANES), F32),
                pltpu.VMEM((halves, tiles, SUB, LANES), F32),
                pltpu.VMEM((bricks * rows_msg, LANES), F32),
                pltpu.VMEM((bricks, rows_msg, LANES), jnp.bfloat16),
                pltpu.SemaphoreType.DMA((3,)),
                pltpu.SemaphoreType.DMA,
                pltpu.SemaphoreType.DMA((4,)),
                pltpu.SemaphoreType.DMA((4,)),
                pltpu.SemaphoreType.DMA,
                pltpu.SemaphoreType.DMA,
                pltpu.SemaphoreType.REGULAR,
                pltpu.SemaphoreType.REGULAR,
            ],
            compiler_params=pltpu.CompilerParams(collective_id=0, has_side_effects=True),
        )(density, tf_bins, tf_table)
        return pl.pallas_call(
            functools.partial(composite, bricks, rows_msg // 4),
            out_shape=jax.ShapeDtypeStruct((4, owned), F32),
            in_specs=[
                pl.BlockSpec(memory_space=pltpu.SMEM),
                pl.BlockSpec(memory_space=pltpu.VMEM),
            ],
            out_specs=pl.BlockSpec(memory_space=pltpu.VMEM),
        )(brick_order, arrived)

    return jax.shard_map(
        per_device,
        mesh=mesh,
        in_specs=(P("depth", "strip", None), P("depth", "strip", None), P(), P("strip", None)),
        out_specs=P(None, ("strip", "depth")),
        check_vma=False,
    )
```

```python
import functools

import jax
import jax.numpy as jnp
from jax import lax
from jax.experimental import pallas as pl
from jax.experimental.pallas import tpu as pltpu
from jax.sharding import PartitionSpec as P

LIGHT_X = 0.36
LIGHT_Y = 0.48
LIGHT_Z = 0.8
SHADE_GAIN = 1.5
MESH = pl.DeviceIdType.MESH
LANES = 128
RING = 8
EARLY = 3
SUB = 8
F32 = jnp.float32


def kernel(
    bricks, strips, planes, height, across, classes,
    dens_hbm, bins_hbm, table_hbm, arrived,
    dens_v, bins_v, table_v, tab, field, rows_out, rows_in, plane_in,
    raw, part_a, part_q, near, far, depth, wide, packed,
    in_sem, own_sem, halo_send, halo_recv, tile_send, tile_recv, late_in, all_in,
):
    me = lax.axis_index("depth")
    strip = lax.axis_index("strip")
    tiles = across // LANES
    halves = height // SUB
    per_owner = height * tiles // bricks
    rows_msg = 4 * per_owner

    cores = 2
    deep = min(RING, bricks // cores)
    rows_x = bricks // (cores * deep)
    core = lax.rem(me, cores)
    z = lax.rem(lax.div(me, cores), deep)
    x = lax.div(me, cores * deep)
    pitch = height + 2 * SUB
    has_below = me > 0
    has_over = me < bricks - 1
    has_upper = strip > 0
    has_lower = strip < strips - 1
    below = lax.rem(me + bricks - 1, bricks)
    over = lax.rem(me + 1, bricks)

    def place(x_to, z_to, core_to):
        return (x_to * deep + z_to) * cores + core_to

    def is_late(index):
        return lax.rem(lax.div(index, cores), deep) >= EARLY + (index < cores * deep).astype(jnp.int32)

    late = is_late(me)
    early = jnp.logical_not(late)
    n_early = (EARLY * rows_x + 1) * cores

    def signal(sem, target):
        pl.semaphore_signal(sem, inc=1, device_id=target, device_id_type=MESH)

    def at(p, t, row, count=SUB):
        start = (p * tiles + t) * pitch + SUB + row
        if not isinstance(start, int) and row % SUB == 0:
            start = pl.multiple_of(start, SUB)
        return pl.ds(start, count)

    def put(p, t, value):
        field[at(p, t, 0, height), :] = value

    def row_of(p, row):
        return pl.ds(p * tiles * pitch + SUB + row, tiles, stride=pitch)

    loads = [
        pltpu.make_async_copy(dens_hbm.at[planes - 1], dens_v.at[planes - 1], in_sem.at[0]),
        pltpu.make_async_copy(dens_hbm.at[0], dens_v.at[0], in_sem.at[1]),
        pltpu.make_async_copy(
            dens_hbm.at[pl.ds(1, planes - 2)], dens_v.at[pl.ds(1, planes - 2)], in_sem.at[2]
        ),
        pltpu.make_async_copy(bins_hbm, bins_v, in_sem.at[3]),
        pltpu.make_async_copy(table_hbm, table_v, in_sem.at[4]),
    ]
    for load in loads:
        load.start()

    barrier = pltpu.get_barrier_semaphore()

    @pl.when(has_upper)
    def _():
        signal(barrier, {"strip": strip - 1})

    @pl.when(has_lower)
    def _():
        signal(barrier, {"strip": strip + 1})

    @pl.when(jnp.logical_and(late, has_below))
    def _():
        signal(barrier, {"depth": below})

    @pl.when(jnp.logical_and(late, has_over))
    def _():
        signal(barrier, {"depth": over})

    @pl.when(early)
    def _():
        def greet(step, carry):
            signal(barrier, {"depth": lax.rem(me + step, bricks)})
            return carry

        lax.fori_loop(1, bricks, greet, 0)

    greeted = (
        n_early
        - early.astype(jnp.int32)
        + has_upper.astype(jnp.int32)
        + has_lower.astype(jnp.int32)
        + jnp.logical_and(has_below, is_late(below)).astype(jnp.int32)
        + jnp.logical_and(has_over, is_late(over)).astype(jnp.int32)
    )

    def halo(src, dst, slot, target):
        return pltpu.make_async_remote_copy(
            src_ref=src, dst_ref=dst, send_sem=halo_send.at[slot], recv_sem=halo_recv.at[slot],
            device_id=target, device_id_type=MESH,
        )

    cut = (tiles // 2 + 1) * LANES
    pieces = (slice(0, cut), slice(cut, across))
    to_over = [
        halo(dens_v.at[planes - 1, :, part], plane_in.at[0, :, part], i, {"depth": over})
        for i, part in enumerate(pieces)
    ]
    to_below = [
        halo(dens_v.at[0, :, part], plane_in.at[1, :, part], 2 + i, {"depth": below})
        for i, part in enumerate(pieces)
    ]
    to_lower = halo(rows_out.at[1], rows_in.at[0], 4, {"strip": lax.rem(strip + 1, strips)})
    to_upper = halo(rows_out.at[0], rows_in.at[1], 5, {"strip": lax.rem(strip + strips - 1, strips)})

    loads[0].wait()
    loads[1].wait()
    loads[2].wait()
    for p in range(planes):
        for t in range(tiles):
            put(p + 1, t, dens_v[p, :, t * LANES : (t + 1) * LANES].astype(F32))
    for p in range(planes):
        rows_out[0, p] = field[row_of(p + 1, 0), :].astype(jnp.bfloat16)
        rows_out[1, p] = field[row_of(p + 1, height - 1), :].astype(jnp.bfloat16)
    pl.semaphore_wait(barrier, greeted)
    pl.when(has_lower)(to_lower.start)
    pl.when(has_upper)(to_upper.start)
    for piece in range(2):
        pl.when(has_over)(to_over[piece].start)
        pl.when(has_below)(to_below[piece].start)

    @pl.when(late)
    def _():
        def report(step, carry):
            z_to = lax.div(step, rows_x * cores)
            signal(late_in, {"depth": place(lax.rem(lax.div(step, cores), rows_x), z_to, lax.rem(step, cores))})
            return carry

        lax.fori_loop(0, n_early, report, 0)

    loads[4].wait()
    tab[0:4, 0:classes] = table_v[...]
    loads[3].wait()

    lane = lax.broadcasted_iota(jnp.int32, (SUB, LANES), 1)
    zero = jnp.zeros((SUB, LANES), F32)
    columns = [jnp.broadcast_to(tab[c : c + 1, :], (SUB, LANES)) for c in range(4)]
    depth[...] = jnp.zeros_like(depth)

    def shear_of(p):
        scaled = 3 * (me * planes + p)
        offset = lax.div(scaled, 8)
        fraction = lax.rem(scaled, 8).astype(F32) * 0.125
        return offset, fraction

    def look_up(p, carry):
        for h in range(halves):
            for t in range(tiles):
                centre = field[at(p + 1, t, SUB * h), :]
                spot = bins_v[p, SUB * h : SUB * h + SUB, t * LANES : (t + 1) * LANES]
                looked = [
                    jnp.take_along_axis(column, spot, axis=1, mode="promise_in_bounds")
                    for column in columns
                ]
                extinction = looked[0] * (1.0 + centre * centre) * (1.0 / (planes * bricks))
                opacity = 1.0 - jnp.exp(-extinction)
                raw[0, h, p, t] = extinction
                for c in range(3):
                    raw[c + 1, h, p, t] = looked[c + 1] * opacity
        return carry

    lax.fori_loop(0, planes, look_up, 0)

    def plane_terms(p, carry):
        offset, fraction = shear_of(p)
        roll_a = lax.rem(LANES - offset, LANES)
        roll_b = LANES - 1 - offset
        mask_a = lane < LANES - offset
        mask_b = lane < LANES - 1 - offset
        for h in range(halves):
            before = [(zero, zero)] * 4
            for t in reversed(range(tiles)):
                centre = field[at(p + 1, t, SUB * h), :]
                right = field[at(p + 1, t + 1, SUB * h), :] if t < tiles - 1 else zero
                left = field[at(p + 1, t - 1, SUB * h), :] if t > 0 else zero
                up = jnp.where(lane < LANES - 1, pltpu.roll(centre, LANES - 1, 1), pltpu.roll(right, LANES - 1, 1))
                down = jnp.where(lane > 0, pltpu.roll(centre, 1, 1), pltpu.roll(left, 1, 1))
                slope = 0.5 * (up - down)
                part_a[h, p, t] = LIGHT_X * slope
                part_q[h, p, t] = 1.0 + slope * slope
                fields = [raw[c, h, p, t] for c in range(4)]
                rolled = [(pltpu.roll(v, roll_a, 1), pltpu.roll(v, roll_b, 1)) for v in fields]
                first = [jnp.where(mask_a, rolled[i][0], before[i][0]) for i in range(4)]
                second = [jnp.where(mask_b, rolled[i][1], before[i][1]) for i in range(4)]
                before = rolled
                sofar = depth[h, t]
                through = jnp.exp(-sofar)
                depth[h, t] = sofar + ((1.0 - fraction) * first[0] + fraction * second[0])
                scale_a = (1.0 - fraction) * through
                scale_b = fraction * through
                for c in range(3):
                    near[c, h, p, t] = scale_a * first[c + 1]
                    far[c, h, p, t] = scale_b * second[c + 1]
        return carry

    lax.fori_loop(0, planes, plane_terms, 0)

    def fill(present, copies, slot, p, piece):
        span = range(pieces[piece].start // LANES, pieces[piece].stop // LANES)

        @pl.when(present)
        def _():
            copies[piece].wait_recv()
            for t in span:
                put(p, t, plane_in[slot, :, t * LANES : (t + 1) * LANES].astype(F32))

        @pl.when(jnp.logical_not(present))
        def _():
            for t in span:
                put(p, t, jnp.zeros((height, LANES), F32))

    def fill_piece(piece):
        fill(has_below, to_over, 0, 0, piece)
        fill(has_over, to_below, 1, planes + 1, piece)

    def border(present, copy, slot, row):
        @pl.when(present)
        def _():
            copy.wait_recv()
            for p in range(planes):
                field[row_of(p + 1, row), :] = rows_in[slot, p].astype(F32)

        @pl.when(jnp.logical_not(present))
        def _():
            for p in range(planes):
                field[row_of(p + 1, row), :] = jnp.zeros((tiles, LANES), F32)

    fill_piece(0)
    border(has_upper, to_lower, 0, -1)
    border(has_lower, to_upper, 1, height)

    def tile_copy(owner):
        return pltpu.make_async_remote_copy(
            src_ref=packed.at[owner], dst_ref=arrived.at[me], send_sem=tile_send, recv_sem=tile_recv,
            device_id={"depth": owner}, device_id_type=MESH,
        )

    def send(z_to, carry):
        for x_to in range(rows_x):
            for core_to in reversed(range(cores)):
                owner = place(x_to, z_to, core_to)
                pl.when(owner != me)(tile_copy(owner).start)
        return carry

    shears = [shear_of(p) for p in range(planes)]
    split = tiles // 2 if 4 * per_owner == tiles else 0

    def shade(low, high):
        for h in range(halves):
            before = [(zero, zero)] * planes
            for t in reversed(range(low, min(high + 1, tiles))):
                colour = [zero] * 3
                for p in range(planes):
                    offset = shears[p][0]
                    row = SUB * h
                    slope_down = 0.5 * (field[at(p + 1, t, row + 1), :] - field[at(p + 1, t, row - 1), :])
                    slope_deep = 0.5 * (field[at(p + 2, t, row), :] - field[at(p, t, row), :])
                    square = part_q[h, p, t] + slope_down * slope_down + slope_deep * slope_deep
                    toward = part_a[h, p, t] + LIGHT_Y * slope_down + LIGHT_Z * slope_deep
                    gain = jnp.exp(SHADE_GAIN * toward * lax.rsqrt(square))
                    gain_a = pltpu.roll(gain, lax.rem(LANES - offset, LANES), 1)
                    gain_b = pltpu.roll(gain, LANES - 1 - offset, 1)
                    if t < high:
                        first = jnp.where(lane < LANES - offset, gain_a, before[p][0])
                        second = jnp.where(lane < LANES - 1 - offset, gain_b, before[p][1])
                        for c in range(3):
                            colour[c] = colour[c] + (near[c, h, p, t] * first + far[c, h, p, t] * second)
                    before[p] = (gain_a, gain_b)
                if t < high:
                    spot = SUB * h * tiles + t
                    start = spot // per_owner * rows_msg + spot % per_owner
                    for c, value in enumerate(colour + [depth[h, t]]):
                        wide[pl.ds(start + c * per_owner, SUB, stride=tiles * 4), :] = value

    def pack(owners):
        for owner in owners:
            packed[owner] = wide[owner * rows_msg : (owner + 1) * rows_msg, :].astype(jnp.bfloat16)

    def in_ring(owner):
        return owner // cores % deep

    everyone_else = [owner for owner in range(bricks) if in_ring(owner) != 0]
    if split:
        shade(0, split)
    else:
        fill_piece(1)
        shade(0, tiles)
    pack([owner for owner in range(bricks) if in_ring(owner) == 0])
    send(0, 0)
    if split:
        fill_piece(1)
        shade(split, tiles)
    pack(everyone_else)
    lax.fori_loop(1, EARLY, send, 0)
    for core_to in range(cores):
        owner = place(0, EARLY, core_to)
        pl.when(owner != me)(tile_copy(owner).start)

    @pl.when(early)
    def _():
        pl.semaphore_wait(late_in, bricks - n_early)
        wide_row = x == 0
        thin_row = x > 0
        for chosen, targets in (
            (z == 0, (deep - 1, deep - 2)),
            (jnp.logical_and(thin_row, z == EARLY - 1), (EARLY, EARLY + 1, EARLY + 2)),
            (jnp.logical_and(wide_row, z == EARLY), (EARLY + 1, EARLY + 2)),
        ):

            @pl.when(chosen)
            def _(targets=targets):
                for target in targets:
                    signal(all_in, {"depth": place(x, target, core)})

    @pl.when(late)
    def _():
        pl.semaphore_wait(all_in, 1)

    for step in range(1, rows_x):
        for core_to in range(cores):
            owner = place(step, EARLY, core_to)
            pl.when(owner != me)(tile_copy(owner).start)
    lax.fori_loop(EARLY + 1, deep, send, 0)

    own = pltpu.make_async_copy(packed.at[me], arrived.at[me], own_sem)
    own.start()
    own.wait()
    for piece in range(2):
        pl.when(has_over)(to_over[piece].wait_send)
        pl.when(has_below)(to_below[piece].wait_send)
    pl.when(has_lower)(to_lower.wait_send)
    pl.when(has_upper)(to_upper.wait_send)
    everyone = pltpu.make_async_remote_copy(
        src_ref=packed.at[pl.ds(0, bricks - 1)], dst_ref=arrived.at[pl.ds(0, bricks - 1)],
        send_sem=tile_send, recv_sem=tile_recv,
        device_id={"depth": lax.rem(me + 1, bricks)}, device_id_type=MESH,
    )
    everyone.wait_recv()

    everyone.wait_send()


def composite(bricks, per_owner, order, arrived, out_ref):
    rows_msg = 4 * per_owner
    row = lax.broadcasted_iota(jnp.int32, (rows_msg, LANES), 0)
    last = row >= 3 * per_owner

    group = min(bricks, 32)

    def layer(slot, carry):
        shown, prefix = carry
        for inner in range(group):
            tile = arrived[order[0, slot * group + inner]].astype(F32)
            shown = shown + jnp.exp(-prefix) * tile
            spread = jnp.where(last, tile, 0.0)
            spread = spread + pltpu.roll(spread, 2 * per_owner, 0)
            spread = spread + pltpu.roll(spread, per_owner, 0)
            prefix = prefix + spread
        return shown, prefix

    blank = jnp.zeros((rows_msg, LANES), F32)
    shown, prefix = lax.fori_loop(0, bricks // group, layer, (blank, blank))
    shown = jnp.where(last, jnp.exp(-prefix), shown)
    for r in range(rows_msg):
        c, piece = r // per_owner, r % per_owner
        out_ref[c : c + 1, piece * LANES : (piece + 1) * LANES] = shown[r : r + 1, :]


def solution(mesh):
    bricks = mesh.shape["depth"]
    strips = mesh.shape["strip"]

    def per_device(density, tf_bins, tf_table, brick_order):
        planes, height, across = density.shape
        classes = tf_table.shape[1]
        tiles = across // LANES
        halves = height // SUB
        owned = height * across // bricks
        rows_msg = 4 * owned // LANES
        arrived = pl.pallas_call(
            functools.partial(kernel, bricks, strips, planes, height, across, classes),
            out_shape=jax.ShapeDtypeStruct((bricks, rows_msg, LANES), jnp.bfloat16),
            in_specs=[pl.BlockSpec(memory_space=pl.ANY)] * 3,
            out_specs=pl.BlockSpec(memory_space=pl.ANY),
            scratch_shapes=[
                pltpu.VMEM((planes, height, across), jnp.bfloat16),
                pltpu.VMEM((planes, height, across), jnp.int32),
                pltpu.VMEM((4, classes), F32),
                pltpu.VMEM((SUB, LANES), F32),
                pltpu.VMEM(((planes + 2) * tiles * (height + 2 * SUB), LANES), F32),
                pltpu.VMEM((2, planes, tiles, LANES), jnp.bfloat16),
                pltpu.VMEM((2, planes, tiles, LANES), jnp.bfloat16),
                pltpu.VMEM((2, height, across), jnp.bfloat16),
                pltpu.VMEM((4, halves, planes, tiles, SUB, LANES), F32),
                pltpu.VMEM((halves, planes, tiles, SUB, LANES), F32),
                pltpu.VMEM((halves, planes, tiles, SUB, LANES), F32),
                pltpu.VMEM((3, halves, planes, tiles, SUB, LANES), F32),
                pltpu.VMEM((3, halves, planes, tiles, SUB, LANES), F32),
                pltpu.VMEM((halves, tiles, SUB, LANES), F32),
                pltpu.VMEM((bricks * rows_msg, LANES), F32),
                pltpu.VMEM((bricks, rows_msg, LANES), jnp.bfloat16),
                pltpu.SemaphoreType.DMA((5,)),
                pltpu.SemaphoreType.DMA,
                pltpu.SemaphoreType.DMA((6,)),
                pltpu.SemaphoreType.DMA((6,)),
                pltpu.SemaphoreType.DMA,
                pltpu.SemaphoreType.DMA,
                pltpu.SemaphoreType.REGULAR,
                pltpu.SemaphoreType.REGULAR,
            ],
            compiler_params=pltpu.CompilerParams(collective_id=0, has_side_effects=True),
        )(density, tf_bins, tf_table)
        return pl.pallas_call(
            functools.partial(composite, bricks, rows_msg // 4),
            out_shape=jax.ShapeDtypeStruct((4, owned), F32),
            in_specs=[
                pl.BlockSpec(memory_space=pltpu.SMEM),
                pl.BlockSpec(memory_space=pltpu.VMEM),
            ],
            out_specs=pl.BlockSpec(memory_space=pltpu.VMEM),
        )(brick_order, arrived)

    return jax.shard_map(
        per_device,
        mesh=mesh,
        in_specs=(P("depth", "strip", None), P("depth", "strip", None), P(), P("strip", None)),
        out_specs=P(None, ("strip", "depth")),
        check_vma=False,
    )
```

```python
import functools

import jax
import jax.numpy as jnp
from jax import lax
from jax.experimental import pallas as pl
from jax.experimental.pallas import tpu as pltpu
from jax.sharding import PartitionSpec as P

LIGHT_X = 0.36
LIGHT_Y = 0.48
LIGHT_Z = 0.8
SHADE_GAIN = 1.5
MESH = pl.DeviceIdType.MESH
LANES = 128
RING = 8
EARLY = 3
SUB = 8
F32 = jnp.float32


def kernel(
    bricks, strips, planes, height, across, classes,
    dens_hbm, bins_hbm, table_hbm, arrived,
    dens_v, bins_v, table_v, tab, field, rows_out, rows_in, plane_in,
    raw, part_a, part_q, near, far, depth, wide, packed,
    in_sem, own_sem, halo_send, halo_recv, tile_send, tile_recv, late_in, all_in,
):
    me = lax.axis_index("depth")
    strip = lax.axis_index("strip")
    tiles = across // LANES
    halves = height // SUB
    per_owner = height * tiles // bricks
    rows_msg = 4 * per_owner

    cores = 2
    deep = min(RING, bricks // cores)
    rows_x = bricks // (cores * deep)
    core = lax.rem(me, cores)
    z = lax.rem(lax.div(me, cores), deep)
    x = lax.div(me, cores * deep)
    pitch = height + 2 * SUB
    has_below = me > 0
    has_over = me < bricks - 1
    has_upper = strip > 0
    has_lower = strip < strips - 1
    below = lax.rem(me + bricks - 1, bricks)
    over = lax.rem(me + 1, bricks)

    def place(x_to, z_to, core_to):
        return (x_to * deep + z_to) * cores + core_to

    def is_late(index):
        return lax.rem(lax.div(index, cores), deep) >= EARLY + (index < cores * deep).astype(jnp.int32)

    late = is_late(me)
    early = jnp.logical_not(late)
    n_early = (EARLY * rows_x + 1) * cores

    def signal(sem, target):
        pl.semaphore_signal(sem, inc=1, device_id=target, device_id_type=MESH)

    def at(p, t, row, count=SUB):
        start = (p * tiles + t) * pitch + SUB + row
        if not isinstance(start, int) and row % SUB == 0:
            start = pl.multiple_of(start, SUB)
        return pl.ds(start, count)

    def put(p, t, value):
        field[at(p, t, 0, height), :] = value

    def row_of(p, row):
        return pl.ds(p * tiles * pitch + SUB + row, tiles, stride=pitch)

    loads = [
        pltpu.make_async_copy(dens_hbm.at[planes - 1], dens_v.at[planes - 1], in_sem.at[0]),
        pltpu.make_async_copy(dens_hbm.at[0], dens_v.at[0], in_sem.at[1]),
        pltpu.make_async_copy(
            dens_hbm.at[pl.ds(1, planes - 2)], dens_v.at[pl.ds(1, planes - 2)], in_sem.at[2]
        ),
        pltpu.make_async_copy(bins_hbm, bins_v, in_sem.at[3]),
        pltpu.make_async_copy(table_hbm, table_v, in_sem.at[4]),
    ]
    for load in loads:
        load.start()

    barrier = pltpu.get_barrier_semaphore()

    @pl.when(has_upper)
    def _():
        signal(barrier, {"strip": strip - 1})

    @pl.when(has_lower)
    def _():
        signal(barrier, {"strip": strip + 1})

    @pl.when(jnp.logical_and(late, has_below))
    def _():
        signal(barrier, {"depth": below})

    @pl.when(jnp.logical_and(late, has_over))
    def _():
        signal(barrier, {"depth": over})

    @pl.when(early)
    def _():
        def greet(step, carry):
            signal(barrier, {"depth": lax.rem(me + step, bricks)})
            return carry

        lax.fori_loop(1, bricks, greet, 0)

    greeted = (
        n_early
        - early.astype(jnp.int32)
        + has_upper.astype(jnp.int32)
        + has_lower.astype(jnp.int32)
        + jnp.logical_and(has_below, is_late(below)).astype(jnp.int32)
        + jnp.logical_and(has_over, is_late(over)).astype(jnp.int32)
    )

    def halo(src, dst, slot, target):
        return pltpu.make_async_remote_copy(
            src_ref=src, dst_ref=dst, send_sem=halo_send.at[slot], recv_sem=halo_recv.at[slot],
            device_id=target, device_id_type=MESH,
        )

    cut = (tiles // 2 + 1) * LANES
    pieces = (
        (slice(0, SUB), slice(0, cut)),
        (slice(SUB, height), slice(0, cut)),
        (slice(0, height), slice(cut, across)),
    )
    to_over = [
        halo(dens_v.at[planes - 1, *part], plane_in.at[0, *part], i, {"depth": over})
        for i, part in enumerate(pieces)
    ]
    to_below = [
        halo(dens_v.at[0, *part], plane_in.at[1, *part], 3 + i, {"depth": below})
        for i, part in enumerate(pieces)
    ]
    to_lower = halo(rows_out.at[1], rows_in.at[0], 6, {"strip": lax.rem(strip + 1, strips)})
    to_upper = halo(rows_out.at[0], rows_in.at[1], 7, {"strip": lax.rem(strip + strips - 1, strips)})

    loads[0].wait()
    loads[1].wait()
    loads[2].wait()
    for p in range(planes):
        for t in range(tiles):
            put(p + 1, t, dens_v[p, :, t * LANES : (t + 1) * LANES].astype(F32))
    for p in range(planes):
        rows_out[0, p] = field[row_of(p + 1, 0), :].astype(jnp.bfloat16)
        rows_out[1, p] = field[row_of(p + 1, height - 1), :].astype(jnp.bfloat16)
    pl.semaphore_wait(barrier, greeted)
    pl.when(has_lower)(to_lower.start)
    pl.when(has_upper)(to_upper.start)
    for piece in range(len(pieces)):
        pl.when(has_over)(to_over[piece].start)
        pl.when(has_below)(to_below[piece].start)

    @pl.when(late)
    def _():
        def report(step, carry):
            z_to = lax.div(step, rows_x * cores)
            signal(late_in, {"depth": place(lax.rem(lax.div(step, cores), rows_x), z_to, lax.rem(step, cores))})
            return carry

        lax.fori_loop(0, n_early, report, 0)

    loads[4].wait()
    tab[0:4, 0:classes] = table_v[...]
    loads[3].wait()

    lane = lax.broadcasted_iota(jnp.int32, (SUB, LANES), 1)
    zero = jnp.zeros((SUB, LANES), F32)
    columns = [jnp.broadcast_to(tab[c : c + 1, :], (SUB, LANES)) for c in range(4)]
    depth[...] = jnp.zeros_like(depth)

    def shear_of(p):
        scaled = 3 * (me * planes + p)
        offset = lax.div(scaled, 8)
        fraction = lax.rem(scaled, 8).astype(F32) * 0.125
        return offset, fraction

    def look_up(p, carry):
        for h in range(halves):
            for t in range(tiles):
                centre = field[at(p + 1, t, SUB * h), :]
                spot = bins_v[p, SUB * h : SUB * h + SUB, t * LANES : (t + 1) * LANES]
                looked = [
                    jnp.take_along_axis(column, spot, axis=1, mode="promise_in_bounds")
                    for column in columns
                ]
                extinction = looked[0] * (1.0 + centre * centre) * (1.0 / (planes * bricks))
                opacity = 1.0 - jnp.exp(-extinction)
                raw[0, h, p, t] = extinction
                for c in range(3):
                    raw[c + 1, h, p, t] = looked[c + 1] * opacity
        return carry

    lax.fori_loop(0, planes, look_up, 0)

    def plane_terms(p, carry):
        offset, fraction = shear_of(p)
        roll_a = lax.rem(LANES - offset, LANES)
        roll_b = LANES - 1 - offset
        mask_a = lane < LANES - offset
        mask_b = lane < LANES - 1 - offset
        for h in range(halves):
            before = [(zero, zero)] * 4
            for t in reversed(range(tiles)):
                centre = field[at(p + 1, t, SUB * h), :]
                right = field[at(p + 1, t + 1, SUB * h), :] if t < tiles - 1 else zero
                left = field[at(p + 1, t - 1, SUB * h), :] if t > 0 else zero
                up = jnp.where(lane < LANES - 1, pltpu.roll(centre, LANES - 1, 1), pltpu.roll(right, LANES - 1, 1))
                down = jnp.where(lane > 0, pltpu.roll(centre, 1, 1), pltpu.roll(left, 1, 1))
                slope = 0.5 * (up - down)
                part_a[h, p, t] = LIGHT_X * slope
                part_q[h, p, t] = 1.0 + slope * slope
                fields = [raw[c, h, p, t] for c in range(4)]
                rolled = [(pltpu.roll(v, roll_a, 1), pltpu.roll(v, roll_b, 1)) for v in fields]
                first = [jnp.where(mask_a, rolled[i][0], before[i][0]) for i in range(4)]
                second = [jnp.where(mask_b, rolled[i][1], before[i][1]) for i in range(4)]
                before = rolled
                sofar = depth[h, t]
                through = jnp.exp(-sofar)
                depth[h, t] = sofar + ((1.0 - fraction) * first[0] + fraction * second[0])
                scale_a = (1.0 - fraction) * through
                scale_b = fraction * through
                for c in range(3):
                    near[c, h, p, t] = scale_a * first[c + 1]
                    far[c, h, p, t] = scale_b * second[c + 1]
        return carry

    lax.fori_loop(0, planes, plane_terms, 0)

    def fill(present, copies, slot, p, piece):
        rows, columns = pieces[piece]
        span = range(columns.start // LANES, columns.stop // LANES)
        count = rows.stop - rows.start

        @pl.when(present)
        def _():
            copies[piece].wait_recv()
            for t in span:
                field[at(p, t, rows.start, count), :] = plane_in[
                    slot, rows, t * LANES : (t + 1) * LANES
                ].astype(F32)

        @pl.when(jnp.logical_not(present))
        def _():
            for t in span:
                field[at(p, t, rows.start, count), :] = jnp.zeros((count, LANES), F32)

    def fill_piece(piece):
        fill(has_below, to_over, 0, 0, piece)
        fill(has_over, to_below, 1, planes + 1, piece)

    def border(present, copy, slot, row):
        @pl.when(present)
        def _():
            copy.wait_recv()
            for p in range(planes):
                field[row_of(p + 1, row), :] = rows_in[slot, p].astype(F32)

        @pl.when(jnp.logical_not(present))
        def _():
            for p in range(planes):
                field[row_of(p + 1, row), :] = jnp.zeros((tiles, LANES), F32)


    def tile_copy(owner):
        return pltpu.make_async_remote_copy(
            src_ref=packed.at[owner], dst_ref=arrived.at[me], send_sem=tile_send, recv_sem=tile_recv,
            device_id={"depth": owner}, device_id_type=MESH,
        )

    def send(z_to, carry):
        for x_to in range(rows_x):
            for core_to in reversed(range(cores)):
                owner = place(x_to, z_to, core_to)
                pl.when(owner != me)(tile_copy(owner).start)
        return carry

    shears = [shear_of(p) for p in range(planes)]
    split = tiles // 2 if 4 * per_owner == tiles else 0

    def shade(low, high, chosen):
        for h in chosen:
            before = [(zero, zero)] * planes
            for t in reversed(range(low, min(high + 1, tiles))):
                colour = [zero] * 3
                for p in range(planes):
                    offset = shears[p][0]
                    row = SUB * h
                    slope_down = 0.5 * (field[at(p + 1, t, row + 1), :] - field[at(p + 1, t, row - 1), :])
                    slope_deep = 0.5 * (field[at(p + 2, t, row), :] - field[at(p, t, row), :])
                    square = part_q[h, p, t] + slope_down * slope_down + slope_deep * slope_deep
                    toward = part_a[h, p, t] + LIGHT_Y * slope_down + LIGHT_Z * slope_deep
                    gain = jnp.exp(SHADE_GAIN * toward * lax.rsqrt(square))
                    gain_a = pltpu.roll(gain, lax.rem(LANES - offset, LANES), 1)
                    gain_b = pltpu.roll(gain, LANES - 1 - offset, 1)
                    if t < high:
                        first = jnp.where(lane < LANES - offset, gain_a, before[p][0])
                        second = jnp.where(lane < LANES - 1 - offset, gain_b, before[p][1])
                        for c in range(3):
                            colour[c] = colour[c] + (near[c, h, p, t] * first + far[c, h, p, t] * second)
                    before[p] = (gain_a, gain_b)
                if t < high:
                    spot = SUB * h * tiles + t
                    start = spot // per_owner * rows_msg + spot % per_owner
                    for c, value in enumerate(colour + [depth[h, t]]):
                        wide[pl.ds(start + c * per_owner, SUB, stride=tiles * 4), :] = value

    def pack(owners):
        for owner in owners:
            packed[owner] = wide[owner * rows_msg : (owner + 1) * rows_msg, :].astype(jnp.bfloat16)

    def in_ring(owner):
        return owner // cores % deep

    def first_owners(spot):
        return [
            place(x_to, 0, core_to)
            for x_to in range(rows_x)
            for core_to in reversed(range(cores))
            if place(x_to, 0, core_to) * per_owner // (SUB * tiles) == spot
        ]

    def send_first(spot):
        pack(first_owners(spot))
        for owner in first_owners(spot):
            pl.when(owner != me)(tile_copy(owner).start)

    if split:
        fill_piece(0)
        border(has_upper, to_lower, 0, -1)
        shade(0, split, (0,))
        send_first(0)
        fill_piece(1)
        border(has_lower, to_upper, 1, height)
        shade(0, split, (1,))
        send_first(1)
        fill_piece(2)
        shade(split, tiles, range(halves))
    else:
        for piece in range(len(pieces)):
            fill_piece(piece)
        border(has_upper, to_lower, 0, -1)
        border(has_lower, to_upper, 1, height)
        shade(0, tiles, range(halves))
        send_first(0)
        send_first(1)
    pack([owner for owner in range(bricks) if in_ring(owner) != 0])
    lax.fori_loop(1, EARLY, send, 0)
    for core_to in range(cores):
        owner = place(0, EARLY, core_to)
        pl.when(owner != me)(tile_copy(owner).start)

    @pl.when(early)
    def _():
        pl.semaphore_wait(late_in, bricks - n_early)
        wide_row = x == 0
        thin_row = x > 0
        for chosen, targets in (
            (z == 0, (deep - 1, deep - 2)),
            (jnp.logical_and(thin_row, z == EARLY - 1), (EARLY, EARLY + 1, EARLY + 2)),
            (jnp.logical_and(wide_row, z == EARLY), (EARLY + 1, EARLY + 2)),
        ):

            @pl.when(chosen)
            def _(targets=targets):
                for target in targets:
                    signal(all_in, {"depth": place(x, target, core)})

    @pl.when(late)
    def _():
        pl.semaphore_wait(all_in, 1)

    for step in range(1, rows_x):
        for core_to in range(cores):
            owner = place(step, EARLY, core_to)
            pl.when(owner != me)(tile_copy(owner).start)
    lax.fori_loop(EARLY + 1, deep, send, 0)

    own = pltpu.make_async_copy(packed.at[me], arrived.at[me], own_sem)
    own.start()
    own.wait()
    for piece in range(len(pieces)):
        pl.when(has_over)(to_over[piece].wait_send)
        pl.when(has_below)(to_below[piece].wait_send)
    pl.when(has_lower)(to_lower.wait_send)
    pl.when(has_upper)(to_upper.wait_send)
    everyone = pltpu.make_async_remote_copy(
        src_ref=packed.at[pl.ds(0, bricks - 1)], dst_ref=arrived.at[pl.ds(0, bricks - 1)],
        send_sem=tile_send, recv_sem=tile_recv,
        device_id={"depth": lax.rem(me + 1, bricks)}, device_id_type=MESH,
    )
    everyone.wait_recv()

    everyone.wait_send()


def composite(bricks, per_owner, order, arrived, out_ref):
    rows_msg = 4 * per_owner
    row = lax.broadcasted_iota(jnp.int32, (rows_msg, LANES), 0)
    last = row >= 3 * per_owner

    group = min(bricks, 32)

    def layer(slot, carry):
        shown, prefix = carry
        for inner in range(group):
            tile = arrived[order[0, slot * group + inner]].astype(F32)
            shown = shown + jnp.exp(-prefix) * tile
            spread = jnp.where(last, tile, 0.0)
            spread = spread + pltpu.roll(spread, 2 * per_owner, 0)
            spread = spread + pltpu.roll(spread, per_owner, 0)
            prefix = prefix + spread
        return shown, prefix

    blank = jnp.zeros((rows_msg, LANES), F32)
    shown, prefix = lax.fori_loop(0, bricks // group, layer, (blank, blank))
    shown = jnp.where(last, jnp.exp(-prefix), shown)
    for r in range(rows_msg):
        c, piece = r // per_owner, r % per_owner
        out_ref[c : c + 1, piece * LANES : (piece + 1) * LANES] = shown[r : r + 1, :]


def solution(mesh):
    bricks = mesh.shape["depth"]
    strips = mesh.shape["strip"]

    def per_device(density, tf_bins, tf_table, brick_order):
        planes, height, across = density.shape
        classes = tf_table.shape[1]
        tiles = across // LANES
        halves = height // SUB
        owned = height * across // bricks
        rows_msg = 4 * owned // LANES
        arrived = pl.pallas_call(
            functools.partial(kernel, bricks, strips, planes, height, across, classes),
            out_shape=jax.ShapeDtypeStruct((bricks, rows_msg, LANES), jnp.bfloat16),
            in_specs=[pl.BlockSpec(memory_space=pl.ANY)] * 3,
            out_specs=pl.BlockSpec(memory_space=pl.ANY),
            scratch_shapes=[
                pltpu.VMEM((planes, height, across), jnp.bfloat16),
                pltpu.VMEM((planes, height, across), jnp.int32),
                pltpu.VMEM((4, classes), F32),
                pltpu.VMEM((SUB, LANES), F32),
                pltpu.VMEM(((planes + 2) * tiles * (height + 2 * SUB), LANES), F32),
                pltpu.VMEM((2, planes, tiles, LANES), jnp.bfloat16),
                pltpu.VMEM((2, planes, tiles, LANES), jnp.bfloat16),
                pltpu.VMEM((2, height, across), jnp.bfloat16),
                pltpu.VMEM((4, halves, planes, tiles, SUB, LANES), F32),
                pltpu.VMEM((halves, planes, tiles, SUB, LANES), F32),
                pltpu.VMEM((halves, planes, tiles, SUB, LANES), F32),
                pltpu.VMEM((3, halves, planes, tiles, SUB, LANES), F32),
                pltpu.VMEM((3, halves, planes, tiles, SUB, LANES), F32),
                pltpu.VMEM((halves, tiles, SUB, LANES), F32),
                pltpu.VMEM((bricks * rows_msg, LANES), F32),
                pltpu.VMEM((bricks, rows_msg, LANES), jnp.bfloat16),
                pltpu.SemaphoreType.DMA((5,)),
                pltpu.SemaphoreType.DMA,
                pltpu.SemaphoreType.DMA((8,)),
                pltpu.SemaphoreType.DMA((8,)),
                pltpu.SemaphoreType.DMA,
                pltpu.SemaphoreType.DMA,
                pltpu.SemaphoreType.REGULAR,
                pltpu.SemaphoreType.REGULAR,
            ],
            compiler_params=pltpu.CompilerParams(collective_id=0, has_side_effects=True),
        )(density, tf_bins, tf_table)
        return pl.pallas_call(
            functools.partial(composite, bricks, rows_msg // 4),
            out_shape=jax.ShapeDtypeStruct((4, owned), F32),
            in_specs=[
                pl.BlockSpec(memory_space=pltpu.SMEM),
                pl.BlockSpec(memory_space=pltpu.VMEM),
            ],
            out_specs=pl.BlockSpec(memory_space=pltpu.VMEM),
        )(brick_order, arrived)

    return jax.shard_map(
        per_device,
        mesh=mesh,
        in_specs=(P("depth", "strip", None), P("depth", "strip", None), P(), P("strip", None)),
        out_specs=P(None, ("strip", "depth")),
        check_vma=False,
    )
```

```python
import functools

import jax
import jax.numpy as jnp
from jax import lax
from jax.experimental import pallas as pl
from jax.experimental.pallas import tpu as pltpu
from jax.sharding import PartitionSpec as P

LIGHT_X = 0.36
LIGHT_Y = 0.48
LIGHT_Z = 0.8
SHADE_GAIN = 1.5
MESH = pl.DeviceIdType.MESH
LANES = 128
RING = 8
EARLY = 3
SUB = 8
F32 = jnp.float32


def kernel(
    bricks, strips, planes, height, across, classes,
    dens_hbm, bins_hbm, table_hbm, arrived,
    dens_v, bins_v, table_v, tab, field, rows_out, rows_in, plane_in,
    raw, part_a, part_q, near, far, depth, wide, packed,
    in_sem, own_sem, halo_send, halo_recv, tile_send, tile_recv, late_in, all_in,
):
    me = lax.axis_index("depth")
    strip = lax.axis_index("strip")
    tiles = across // LANES
    halves = height // SUB
    per_owner = height * tiles // bricks
    rows_msg = 4 * per_owner

    cores = 2
    deep = min(RING, bricks // cores)
    rows_x = bricks // (cores * deep)
    core = lax.rem(me, cores)
    z = lax.rem(lax.div(me, cores), deep)
    x = lax.div(me, cores * deep)
    pitch = height + 2 * SUB
    has_below = me > 0
    has_over = me < bricks - 1
    has_upper = strip > 0
    has_lower = strip < strips - 1
    below = lax.rem(me + bricks - 1, bricks)
    over = lax.rem(me + 1, bricks)

    def place(x_to, z_to, core_to):
        return (x_to * deep + z_to) * cores + core_to

    def is_late(index):
        return lax.rem(lax.div(index, cores), deep) >= EARLY + (index < cores * deep).astype(jnp.int32)

    late = is_late(me)
    early = jnp.logical_not(late)
    n_early = (EARLY * rows_x + 1) * cores

    def signal(sem, target):
        pl.semaphore_signal(sem, inc=1, device_id=target, device_id_type=MESH)

    def at(p, t, row, count=SUB):
        start = (p * tiles + t) * pitch + SUB + row
        if not isinstance(start, int) and row % SUB == 0:
            start = pl.multiple_of(start, SUB)
        return pl.ds(start, count)

    def put(p, t, value):
        field[at(p, t, 0, height), :] = value

    def row_of(p, row):
        return pl.ds(p * tiles * pitch + SUB + row, tiles, stride=pitch)

    loads = [
        pltpu.make_async_copy(dens_hbm.at[planes - 1], dens_v.at[planes - 1], in_sem.at[0]),
        pltpu.make_async_copy(dens_hbm.at[0], dens_v.at[0], in_sem.at[1]),
        pltpu.make_async_copy(
            dens_hbm.at[pl.ds(1, planes - 2)], dens_v.at[pl.ds(1, planes - 2)], in_sem.at[2]
        ),
        pltpu.make_async_copy(bins_hbm, bins_v, in_sem.at[3]),
        pltpu.make_async_copy(table_hbm, table_v, in_sem.at[4]),
    ]
    for load in loads[:3]:
        load.start()

    barrier = pltpu.get_barrier_semaphore()

    @pl.when(has_upper)
    def _():
        signal(barrier, {"strip": strip - 1})

    @pl.when(has_lower)
    def _():
        signal(barrier, {"strip": strip + 1})

    @pl.when(jnp.logical_and(late, has_below))
    def _():
        signal(barrier, {"depth": below})

    @pl.when(jnp.logical_and(late, has_over))
    def _():
        signal(barrier, {"depth": over})

    @pl.when(early)
    def _():
        def greet(step, carry):
            signal(barrier, {"depth": lax.rem(me + step, bricks)})
            return carry

        lax.fori_loop(1, bricks, greet, 0)

    greeted = (
        n_early
        - early.astype(jnp.int32)
        + has_upper.astype(jnp.int32)
        + has_lower.astype(jnp.int32)
        + jnp.logical_and(has_below, is_late(below)).astype(jnp.int32)
        + jnp.logical_and(has_over, is_late(over)).astype(jnp.int32)
    )

    def halo(src, dst, slot, target):
        return pltpu.make_async_remote_copy(
            src_ref=src, dst_ref=dst, send_sem=halo_send.at[slot], recv_sem=halo_recv.at[slot],
            device_id=target, device_id_type=MESH,
        )

    cut = (tiles // 2 + 1) * LANES
    pieces = (
        (slice(0, SUB), slice(0, cut)),
        (slice(SUB, height), slice(0, cut)),
        (slice(0, height), slice(cut, across)),
    )
    to_over = [
        halo(dens_v.at[planes - 1, *part], plane_in.at[0, *part], i, {"depth": over})
        for i, part in enumerate(pieces)
    ]
    to_below = [
        halo(dens_v.at[0, *part], plane_in.at[1, *part], 3 + i, {"depth": below})
        for i, part in enumerate(pieces)
    ]
    to_lower = halo(rows_out.at[1], rows_in.at[0], 6, {"strip": lax.rem(strip + 1, strips)})
    to_upper = halo(rows_out.at[0], rows_in.at[1], 7, {"strip": lax.rem(strip + strips - 1, strips)})

    loads[0].wait()
    loads[1].wait()
    loads[2].wait()
    for load in loads[3:]:
        load.start()
    for p in range(planes):
        for t in range(tiles):
            put(p + 1, t, dens_v[p, :, t * LANES : (t + 1) * LANES].astype(F32))
    for p in range(planes):
        rows_out[0, p] = field[row_of(p + 1, 0), :].astype(jnp.bfloat16)
        rows_out[1, p] = field[row_of(p + 1, height - 1), :].astype(jnp.bfloat16)
    pl.semaphore_wait(barrier, greeted)
    pl.when(has_lower)(to_lower.start)
    pl.when(has_upper)(to_upper.start)
    for piece in range(len(pieces)):
        pl.when(has_over)(to_over[piece].start)
        pl.when(has_below)(to_below[piece].start)

    @pl.when(late)
    def _():
        def report(step, carry):
            z_to = lax.div(step, rows_x * cores)
            signal(late_in, {"depth": place(lax.rem(lax.div(step, cores), rows_x), z_to, lax.rem(step, cores))})
            return carry

        lax.fori_loop(0, n_early, report, 0)

    loads[4].wait()
    tab[0:4, 0:classes] = table_v[...]
    loads[3].wait()

    lane = lax.broadcasted_iota(jnp.int32, (SUB, LANES), 1)
    zero = jnp.zeros((SUB, LANES), F32)
    columns = [jnp.broadcast_to(tab[c : c + 1, :], (SUB, LANES)) for c in range(4)]
    depth[...] = jnp.zeros_like(depth)

    def shear_of(p):
        scaled = 3 * (me * planes + p)
        offset = lax.div(scaled, 8)
        fraction = lax.rem(scaled, 8).astype(F32) * 0.125
        return offset, fraction

    def look_up(p, carry):
        for h in range(halves):
            for t in range(tiles):
                centre = field[at(p + 1, t, SUB * h), :]
                spot = bins_v[p, SUB * h : SUB * h + SUB, t * LANES : (t + 1) * LANES]
                looked = [
                    jnp.take_along_axis(column, spot, axis=1, mode="promise_in_bounds")
                    for column in columns
                ]
                extinction = looked[0] * (1.0 + centre * centre) * (1.0 / (planes * bricks))
                opacity = 1.0 - jnp.exp(-extinction)
                raw[0, h, p, t] = extinction
                for c in range(3):
                    raw[c + 1, h, p, t] = looked[c + 1] * opacity
        return carry

    lax.fori_loop(0, planes, look_up, 0)

    def plane_terms(p, carry):
        offset, fraction = shear_of(p)
        roll_a = lax.rem(LANES - offset, LANES)
        roll_b = LANES - 1 - offset
        mask_a = lane < LANES - offset
        mask_b = lane < LANES - 1 - offset
        for h in range(halves):
            before = [(zero, zero)] * 4
            for t in reversed(range(tiles)):
                centre = field[at(p + 1, t, SUB * h), :]
                right = field[at(p + 1, t + 1, SUB * h), :] if t < tiles - 1 else zero
                left = field[at(p + 1, t - 1, SUB * h), :] if t > 0 else zero
                up = jnp.where(lane < LANES - 1, pltpu.roll(centre, LANES - 1, 1), pltpu.roll(right, LANES - 1, 1))
                down = jnp.where(lane > 0, pltpu.roll(centre, 1, 1), pltpu.roll(left, 1, 1))
                slope = 0.5 * (up - down)
                part_a[h, p, t] = LIGHT_X * slope
                part_q[h, p, t] = 1.0 + slope * slope
                fields = [raw[c, h, p, t] for c in range(4)]
                rolled = [(pltpu.roll(v, roll_a, 1), pltpu.roll(v, roll_b, 1)) for v in fields]
                first = [jnp.where(mask_a, rolled[i][0], before[i][0]) for i in range(4)]
                second = [jnp.where(mask_b, rolled[i][1], before[i][1]) for i in range(4)]
                before = rolled
                sofar = depth[h, t]
                through = jnp.exp(-sofar)
                depth[h, t] = sofar + ((1.0 - fraction) * first[0] + fraction * second[0])
                scale_a = (1.0 - fraction) * through
                scale_b = fraction * through
                for c in range(3):
                    near[c, h, p, t] = scale_a * first[c + 1]
                    far[c, h, p, t] = scale_b * second[c + 1]
        return carry

    lax.fori_loop(0, planes, plane_terms, 0)

    def fill(present, copies, slot, p, piece):
        rows, columns = pieces[piece]
        span = range(columns.start // LANES, columns.stop // LANES)
        count = rows.stop - rows.start

        @pl.when(present)
        def _():
            copies[piece].wait_recv()
            for t in span:
                field[at(p, t, rows.start, count), :] = plane_in[
                    slot, rows, t * LANES : (t + 1) * LANES
                ].astype(F32)

        @pl.when(jnp.logical_not(present))
        def _():
            for t in span:
                field[at(p, t, rows.start, count), :] = jnp.zeros((count, LANES), F32)

    def fill_piece(piece):
        fill(has_below, to_over, 0, 0, piece)
        fill(has_over, to_below, 1, planes + 1, piece)

    def border(present, copy, slot, row):
        @pl.when(present)
        def _():
            copy.wait_recv()
            for p in range(planes):
                field[row_of(p + 1, row), :] = rows_in[slot, p].astype(F32)

        @pl.when(jnp.logical_not(present))
        def _():
            for p in range(planes):
                field[row_of(p + 1, row), :] = jnp.zeros((tiles, LANES), F32)


    def tile_copy(owner):
        return pltpu.make_async_remote_copy(
            src_ref=packed.at[owner], dst_ref=arrived.at[me], send_sem=tile_send, recv_sem=tile_recv,
            device_id={"depth": owner}, device_id_type=MESH,
        )

    def send(z_to, carry):
        for x_to in range(rows_x):
            for core_to in reversed(range(cores)):
                owner = place(x_to, z_to, core_to)
                pl.when(owner != me)(tile_copy(owner).start)
        return carry

    shears = [shear_of(p) for p in range(planes)]
    split = tiles // 2 if 4 * per_owner == tiles else 0

    def shade(low, high, chosen):
        for h in chosen:
            before = [(zero, zero)] * planes
            for t in reversed(range(low, min(high + 1, tiles))):
                colour = [zero] * 3
                for p in range(planes):
                    offset = shears[p][0]
                    row = SUB * h
                    slope_down = 0.5 * (field[at(p + 1, t, row + 1), :] - field[at(p + 1, t, row - 1), :])
                    slope_deep = 0.5 * (field[at(p + 2, t, row), :] - field[at(p, t, row), :])
                    square = part_q[h, p, t] + slope_down * slope_down + slope_deep * slope_deep
                    toward = part_a[h, p, t] + LIGHT_Y * slope_down + LIGHT_Z * slope_deep
                    gain = jnp.exp(SHADE_GAIN * toward * lax.rsqrt(square))
                    gain_a = pltpu.roll(gain, lax.rem(LANES - offset, LANES), 1)
                    gain_b = pltpu.roll(gain, LANES - 1 - offset, 1)
                    if t < high:
                        first = jnp.where(lane < LANES - offset, gain_a, before[p][0])
                        second = jnp.where(lane < LANES - 1 - offset, gain_b, before[p][1])
                        for c in range(3):
                            colour[c] = colour[c] + (near[c, h, p, t] * first + far[c, h, p, t] * second)
                    before[p] = (gain_a, gain_b)
                if t < high:
                    spot = SUB * h * tiles + t
                    start = spot // per_owner * rows_msg + spot % per_owner
                    for c, value in enumerate(colour + [depth[h, t]]):
                        wide[pl.ds(start + c * per_owner, SUB, stride=tiles * 4), :] = value

    def pack(owners):
        for owner in owners:
            packed[owner] = wide[owner * rows_msg : (owner + 1) * rows_msg, :].astype(jnp.bfloat16)

    def in_ring(owner):
        return owner // cores % deep

    def first_owners(spot):
        return [
            place(x_to, 0, core_to)
            for x_to in range(rows_x)
            for core_to in reversed(range(cores))
            if place(x_to, 0, core_to) * per_owner // (SUB * tiles) == spot
        ]

    def send_first(spot, which=(1, 0)):
        chosen = [owner for core_to in which for owner in first_owners(spot) if owner % cores == core_to]
        pack(chosen)
        for owner in chosen:
            pl.when(owner != me)(tile_copy(owner).start)

    if split:
        fill_piece(0)
        border(has_upper, to_lower, 0, -1)
        shade(split // 2, split, (0,))
        send_first(0, (1,))
        shade(0, split // 2, (0,))
        send_first(0, (0,))
        fill_piece(1)
        border(has_lower, to_upper, 1, height)
        shade(0, split, (1,))
        send_first(1)
        fill_piece(2)
        shade(split, tiles, range(halves))
    else:
        for piece in range(len(pieces)):
            fill_piece(piece)
        border(has_upper, to_lower, 0, -1)
        border(has_lower, to_upper, 1, height)
        shade(0, tiles, range(halves))
        send_first(0)
        send_first(1)
    pack([owner for owner in range(bricks) if in_ring(owner) != 0])
    lax.fori_loop(1, EARLY, send, 0)
    for core_to in range(cores):
        owner = place(0, EARLY, core_to)
        pl.when(owner != me)(tile_copy(owner).start)

    @pl.when(early)
    def _():
        pl.semaphore_wait(late_in, bricks - n_early)
        wide_row = x == 0
        thin_row = x > 0
        for chosen, targets in (
            (z == 0, (deep - 1, deep - 2)),
            (jnp.logical_and(thin_row, z == EARLY - 1), (EARLY, EARLY + 1, EARLY + 2)),
            (jnp.logical_and(wide_row, z == EARLY), (EARLY + 1, EARLY + 2)),
        ):

            @pl.when(chosen)
            def _(targets=targets):
                for target in targets:
                    signal(all_in, {"depth": place(x, target, core)})

    @pl.when(late)
    def _():
        pl.semaphore_wait(all_in, 1)

    for step in range(1, rows_x):
        for core_to in range(cores):
            owner = place(step, EARLY, core_to)
            pl.when(owner != me)(tile_copy(owner).start)
    lax.fori_loop(EARLY + 1, deep, send, 0)

    own = pltpu.make_async_copy(packed.at[me], arrived.at[me], own_sem)
    own.start()
    own.wait()
    for piece in range(len(pieces)):
        pl.when(has_over)(to_over[piece].wait_send)
        pl.when(has_below)(to_below[piece].wait_send)
    pl.when(has_lower)(to_lower.wait_send)
    pl.when(has_upper)(to_upper.wait_send)
    everyone = pltpu.make_async_remote_copy(
        src_ref=packed.at[pl.ds(0, bricks - 1)], dst_ref=arrived.at[pl.ds(0, bricks - 1)],
        send_sem=tile_send, recv_sem=tile_recv,
        device_id={"depth": lax.rem(me + 1, bricks)}, device_id_type=MESH,
    )
    everyone.wait_recv()

    everyone.wait_send()


def composite(bricks, per_owner, order, arrived, out_ref):
    rows_msg = 4 * per_owner
    row = lax.broadcasted_iota(jnp.int32, (rows_msg, LANES), 0)
    last = row >= 3 * per_owner

    group = min(bricks, 32)

    def layer(slot, carry):
        shown, prefix = carry
        for inner in range(group):
            tile = arrived[order[0, slot * group + inner]].astype(F32)
            shown = shown + jnp.exp(-prefix) * tile
            spread = jnp.where(last, tile, 0.0)
            spread = spread + pltpu.roll(spread, 2 * per_owner, 0)
            spread = spread + pltpu.roll(spread, per_owner, 0)
            prefix = prefix + spread
        return shown, prefix

    blank = jnp.zeros((rows_msg, LANES), F32)
    shown, prefix = lax.fori_loop(0, bricks // group, layer, (blank, blank))
    shown = jnp.where(last, jnp.exp(-prefix), shown)
    for r in range(rows_msg):
        c, piece = r // per_owner, r % per_owner
        out_ref[c : c + 1, piece * LANES : (piece + 1) * LANES] = shown[r : r + 1, :]


def solution(mesh):
    bricks = mesh.shape["depth"]
    strips = mesh.shape["strip"]

    def per_device(density, tf_bins, tf_table, brick_order):
        planes, height, across = density.shape
        classes = tf_table.shape[1]
        tiles = across // LANES
        halves = height // SUB
        owned = height * across // bricks
        rows_msg = 4 * owned // LANES
        arrived = pl.pallas_call(
            functools.partial(kernel, bricks, strips, planes, height, across, classes),
            out_shape=jax.ShapeDtypeStruct((bricks, rows_msg, LANES), jnp.bfloat16),
            in_specs=[pl.BlockSpec(memory_space=pl.ANY)] * 3,
            out_specs=pl.BlockSpec(memory_space=pl.ANY),
            scratch_shapes=[
                pltpu.VMEM((planes, height, across), jnp.bfloat16),
                pltpu.VMEM((planes, height, across), jnp.int32),
                pltpu.VMEM((4, classes), F32),
                pltpu.VMEM((SUB, LANES), F32),
                pltpu.VMEM(((planes + 2) * tiles * (height + 2 * SUB), LANES), F32),
                pltpu.VMEM((2, planes, tiles, LANES), jnp.bfloat16),
                pltpu.VMEM((2, planes, tiles, LANES), jnp.bfloat16),
                pltpu.VMEM((2, height, across), jnp.bfloat16),
                pltpu.VMEM((4, halves, planes, tiles, SUB, LANES), F32),
                pltpu.VMEM((halves, planes, tiles, SUB, LANES), F32),
                pltpu.VMEM((halves, planes, tiles, SUB, LANES), F32),
                pltpu.VMEM((3, halves, planes, tiles, SUB, LANES), F32),
                pltpu.VMEM((3, halves, planes, tiles, SUB, LANES), F32),
                pltpu.VMEM((halves, tiles, SUB, LANES), F32),
                pltpu.VMEM((bricks * rows_msg, LANES), F32),
                pltpu.VMEM((bricks, rows_msg, LANES), jnp.bfloat16),
                pltpu.SemaphoreType.DMA((5,)),
                pltpu.SemaphoreType.DMA,
                pltpu.SemaphoreType.DMA((8,)),
                pltpu.SemaphoreType.DMA((8,)),
                pltpu.SemaphoreType.DMA,
                pltpu.SemaphoreType.DMA,
                pltpu.SemaphoreType.REGULAR,
                pltpu.SemaphoreType.REGULAR,
            ],
            compiler_params=pltpu.CompilerParams(collective_id=0, has_side_effects=True),
        )(density, tf_bins, tf_table)
        return pl.pallas_call(
            functools.partial(composite, bricks, rows_msg // 4),
            out_shape=jax.ShapeDtypeStruct((4, owned), F32),
            in_specs=[
                pl.BlockSpec(memory_space=pltpu.SMEM),
                pl.BlockSpec(memory_space=pltpu.VMEM),
            ],
            out_specs=pl.BlockSpec(memory_space=pltpu.VMEM),
        )(brick_order, arrived)

    return jax.shard_map(
        per_device,
        mesh=mesh,
        in_specs=(P("depth", "strip", None), P("depth", "strip", None), P(), P("strip", None)),
        out_specs=P(None, ("strip", "depth")),
        check_vma=False,
    )
```
